256 devices in a mesh: clip: 128 (over y_hi, x, z, core), strip: 2 (over y_lo).
Axes of the slice: x: 4, y: 4 (y_hi: 2, y_lo: 2; y = y_hi * 2 + y_lo), z: 8, core: 2. Of those that a mesh axis runs over, the one named last changes fastest.
Arguments:
- video: bfloat16 [256, 2, 32, 32, 256], P('clip', None, 'strip')
- gain_first: float32 [256], replicated, may hold values from 0.1 to 1.9
- conv_weight: bfloat16 [3, 3, 3, 256, 256], replicated, may hold values from -0.078125 to 0.078125
- gain_second: float32 [256], replicated, may hold values from 0.1 to 1.9
- proj_weight: bfloat16 [256, 256], replicated, may hold values from -0.375 to 0.375
- codes: int32 [256, 2, 32, 32], P('clip', None, 'strip'), may hold values from 0 to 1023
- ema_sum: float32 [1024, 256], replicated, may hold values from -12 to 12
- ema_count: float32 [1024], replicated, may hold values from 0.5 to 8
Outputs:
- latent: float32 [256, 2, 32, 32, 256], P('clip', None, 'strip')
- codebook: float32 [1024, 256], replicated
- code_count: float32 [1024], replicated
- clip_error: float32 [256], P('clip')
The draws below stay inside these ranges and needn't reach their ends.
All inputs are finite; a program needn't handle non-finite values.
Results may differ from the reference program's by a relative error of at most 0.0029.
Values may be sent and summed in bfloat16 or wider, within the bound.
A program may use at most 64 MiB of HBM per device.

```python
import math
import jax
import jax.numpy as jnp
import numpy as np
from jax import lax

FRAMES = 2
HGT = 32
WID = 32
CH = 256
EMB = 256
CODES = 1024
GROUPS = 32
CLIPS = 256


def draw_video(key, part):
    noise_key, scale_key = jax.random.split(jax.random.fold_in(key, 11), 2)
    row_scale = jnp.exp(jax.random.uniform(scale_key, (CLIPS, FRAMES, HGT, 1, 1), jnp.float32, 0.0, 2.3))
    values = jax.random.normal(noise_key, (CLIPS, FRAMES, HGT, WID, CH), jnp.float32) * row_scale
    return values.astype(jnp.bfloat16)


def with_ends(values, stream_key, low, high):
    spot = [jax.random.randint(jax.random.fold_in(stream_key, axis), (), 0, length) for axis, length in enumerate(values.shape)]
    longest = values.shape.index(max(values.shape))
    next_to = spot[:longest] + [(spot[longest] + 1) % values.shape[longest]] + spot[longest + 1:]
    return values.at[tuple(spot)].set(low).at[tuple(next_to)].set(high)


def rank_bounds(number_of, lean):
    weights = [(1 << 20) // math.isqrt(grade ** lean) + 1 for grade in range(1, number_of + 1)]
    deviation = 1 + sum(weights) // (1 << 30)
    return np.cumsum(np.array([max(1, weight // deviation) for weight in weights]))


def skewed_ids(rng, extent, count, skew):
    listing = rank_bounds(count, skew)
    pick = jax.random.randint(jax.random.fold_in(rng, 1), extent, 0, int(listing[count - 1]))
    rank = jnp.searchsorted(jnp.asarray(listing, jnp.int32), pick, side="right")
    return jax.random.permutation(jax.random.fold_in(rng, 2), count)[rank].astype(jnp.int32)


def scatter_about(stream_key, extent, deviation, limit, held_as=jnp.bfloat16):
    drawn = jax.random.normal(stream_key, extent, jnp.float32) * deviation
    return jnp.minimum(jnp.maximum(drawn, -limit), limit).astype(held_as)


def setup_inputs(seed: int = 0) -> dict:
    seeds = jax.random.split(jax.random.key(seed), 9)
    return {
        "video": draw_video(jax.random.fold_in(seeds[8], 71), 0),
        "gain_first": jnp.clip(1.0 + 0.18 * jax.random.normal(seeds[1], (CH,), jnp.float32), 0.1, 1.9),
        "conv_weight": scatter_about(seeds[2], (3, 3, 3, CH, CH), (27 * CH) ** -0.5, 0.078125),
        "gain_second": jnp.clip(1.0 + 0.18 * jax.random.normal(seeds[3], (CH,), jnp.float32), 0.1, 1.9),
        "proj_weight": scatter_about(seeds[4], (CH, EMB), CH ** -0.5, 0.375),
        "codes": with_ends(skewed_ids(seeds[5], (CLIPS, FRAMES, HGT, WID), CODES, 3), jax.random.fold_in(seeds[5], 3), 0, CODES - 1).astype(jnp.int32),
        "ema_sum": scatter_about(seeds[6], (CODES, EMB), 2.0, 12.0, jnp.float32),
        "ema_count": jnp.clip(jnp.exp(jax.random.uniform(seeds[7], (CODES,), jnp.float32, math.log(0.5), math.log(8.0))), 0.5, 8.0),
    }


norm_eps = 1e-06
smooth_eps = 1e-05
ema_decay = 0.9

def group_norm(values, gain_vec):
    shaped = values.reshape(values.shape[:4] + (GROUPS, values.shape[4] // GROUPS))
    centre = lax.optimization_barrier(jnp.mean(shaped, axis=(1, 2, 3, 5), keepdims=True))
    spread = lax.optimization_barrier(jnp.mean((shaped - centre) ** 2, axis=(1, 2, 3, 5), keepdims=True))
    normed = (shaped - centre) / jnp.sqrt(spread + norm_eps)
    return normed.reshape(values.shape) * gain_vec

def smoothed_book(sums, counts):
    grand = jnp.sum(counts)
    smooth = (counts + smooth_eps) / (grand + CODES * smooth_eps) * grand
    return sums / smooth[:, None]

def reference(video, gain_first, conv_weight, gain_second, proj_weight, codes, ema_sum, ema_count):
    values = video.astype(jnp.float32)
    act_first = jax.nn.silu(group_norm(values, gain_first)).astype(jnp.bfloat16)
    convolved = lax.conv_general_dilated(act_first, conv_weight, (1, 1, 1), [(2, 0), (1, 1), (1, 1)], dimension_numbers=('NDHWC', 'DHWIO', 'NDHWC'), preferred_element_type=jnp.float32)
    hidden = values + convolved
    act_second = jax.nn.silu(group_norm(hidden, gain_second)).astype(jnp.bfloat16)
    flat_latent = jnp.dot(act_second.reshape(-1, CH), proj_weight, preferred_element_type=jnp.float32)
    flat_codes = codes.reshape(-1)
    old_book = smoothed_book(ema_sum, ema_count)
    quantized = jnp.take(old_book, flat_codes, axis=0)
    squared = lax.optimization_barrier(jnp.sum((flat_latent - quantized) ** 2, axis=1)).reshape(CLIPS, -1)
    clip_error = lax.optimization_barrier(jnp.sum(squared, axis=1)) / (squared.shape[1] * EMB)
    code_sums = jax.ops.segment_sum(flat_latent, flat_codes, CODES)
    token_counts = jax.ops.segment_sum(jnp.ones(flat_codes.shape, jnp.float32), flat_codes, CODES)
    code_count = ema_decay * ema_count + (1.0 - ema_decay) * token_counts
    new_sum = ema_decay * ema_sum + (1.0 - ema_decay) * code_sums
    codebook = smoothed_book(new_sum, code_count)
    latent = flat_latent.reshape(CLIPS, FRAMES, HGT, WID, EMB)
    return (latent, codebook, code_count, clip_error)
```

```python
import functools

import jax
import jax.numpy as jnp
from jax import lax
from jax.experimental import pallas as pl
from jax.experimental.pallas import tpu as pltpu
from jax.sharding import PartitionSpec as P

EMB = 256
CODES = 1024
GROUPS = 32
NORM_EPS = 1e-06
SMOOTH_EPS = 1e-05
DECAY = 0.9
MESH = pl.DeviceIdType.MESH

X, Y, Z, CORES = 4, 4, 8, 2
PLANE = X * Y
HALF = CODES // CORES
CHUNK = HALF // PLANE
bf16, f32 = jnp.bfloat16, jnp.float32


def address(x, y, z, core):
    return (((y // 2 * X + x) * Z + z) * CORES + core, y % 2)


def shifts():
    every = [(dx, dy) for dx in range(X) for dy in range(Y) if dx or dy]
    return sorted(every, key=lambda s: -(min(s[0], X - s[0]) + min(s[1], Y - s[1])))


def z_shifts():
    return sorted(range(1, Z), key=lambda d: -min(d, Z - d))


def kernel(
    video_hbm, weight_hbm, gain1_ref, gain2_ref, proj_ref, codes_ref, ema_sum_hbm, ema_count_ref, ones_ref,
    act_hbm, sums_ref, counts_ref, err_ref,
    vid, halo, weight, wide, hid, act2, member, book, ema_sum, lat,
    stat1, stat2, got1, got2, errs, got_err,
    count_own, count_core, count_chip, count_plane, count_z,
    core_out, core_in, half, plane_in, z_buf,
    load_sem, part_send, part_recv, core_sem,
    rs_send, rs_recv, z_send, z_recv, ag_send, ag_recv, fw_send, fw_recv,
    cp_send, cp_recv, cz_send, cz_recv,
):
    clip, strip = lax.axis_index("clip"), lax.axis_index("strip")
    core = clip % CORES
    z = clip // CORES % Z
    x = clip // (CORES * Z) % X
    y = clip // (CORES * Z * X) * 2 + strip
    clips, frames, rows, cols, ch = vid.shape
    per_frame = rows * cols
    per_clip = frames * per_frame
    steps = shifts()
    z_steps = z_shifts()
    partner = (clip, 1 - strip)
    other_core = address(x, y, z, 1 - core)
    plane_peers = [address((x + dx) % X, (y + dy) % Y, z, core) for dx, dy in steps]
    plane_chunks = [(y + dy) % Y * X + (x + dx) % X for dx, dy in steps]
    from_chunks = [(y - dy + Y) % Y * X + (x - dx + X) % X for dx, dy in steps]
    own_chunk = y * X + x
    z_peers = [address(x, y, (z + d) % Z, core) for d in z_steps]

    barrier = pltpu.get_barrier_semaphore()
    everyone = plane_peers + z_peers + [other_core]
    for peer in everyone:
        pl.semaphore_signal(barrier, inc=1, device_id=peer, device_id_type=MESH)

    load_video = [pltpu.make_async_copy(video_hbm.at[c], vid.at[c], load_sem.at[c]) for c in range(clips)]
    for copy in load_video:
        copy.start()
    taps = weight.shape[0]
    skip = weight_hbm.shape[0] - taps
    load_weight = [
        pltpu.make_async_copy(weight_hbm.at[skip + a], weight.at[a], load_sem.at[clips + a]) for a in range(taps)
    ]
    for copy in load_weight:
        copy.start()
    load_sums = pltpu.make_async_copy(ema_sum_hbm, ema_sum, load_sem.at[clips + taps])
    load_sums.start()

    def remote(src, dst, send, recv, peer):
        return pltpu.make_async_remote_copy(
            src_ref=src, dst_ref=dst, send_sem=send, recv_sem=recv, device_id=peer, device_id_type=MESH
        )

    def fold(v):
        return v.reshape(v.shape[0] // 8, 8, v.shape[1]).sum(axis=0)

    block = 128
    for ref in (stat1, stat2, errs):
        ref[...] = jnp.zeros_like(ref)
    for c in range(clips):
        load_video[c].wait()
        first = second = jnp.zeros((8, ch), f32)
        for t in range(frames):
            def add(i, carry, c=c, t=t):
                r = pl.multiple_of(i * (block // cols), block // cols)
                v = vid[c, t, pl.ds(r, block // cols)].reshape(block, ch).astype(f32)
                return carry[0] + fold(v), carry[1] + fold(v * v)
            first, second = lax.fori_loop(0, per_frame // block, add, (first, second), unroll=True)
        stat1[pl.ds(c, 1)] = first.sum(axis=0, keepdims=True)
        stat1[pl.ds(clips + c, 1)] = second.sum(axis=0, keepdims=True)

    pl.semaphore_wait(barrier, len(everyone))
    edge = (rows - 1) * (1 - strip)
    send_halo = remote(video_hbm.at[:, :, pl.ds(edge, 1)], halo, part_send.at[0], part_recv.at[0], partner)
    send_halo.start()
    send_stat1 = remote(stat1, got1, part_send.at[1], part_recv.at[1], partner)
    send_stat1.start()

    span = 128
    tokens = codes_ref.shape[1]

    def mark(i, carry):
        k = pl.multiple_of(i * span, span)
        number = lax.broadcasted_iota(jnp.int32, (span, 256), 0) + k
        total = jnp.zeros((span, 256), f32)
        for j in range(tokens // 256):
            hit = jnp.where(number == codes_ref[:, j * 256:(j + 1) * 256], 1.0, 0.0)
            total += hit
            member[pl.ds(k, span), j * 256:(j + 1) * 256] = hit.astype(bf16)
        lanes = jnp.broadcast_to(total.sum(axis=1, keepdims=True), (span, span))
        count_own[:, pl.ds(k, span)] = lanes.T[:1]
        return carry

    lax.fori_loop(0, CODES // span, mark, 0)
    send_count = remote(count_own, count_core, core_sem.at[0], core_sem.at[1], other_core)
    send_count.start()

    members = per_clip * 2 * (ch // GROUPS)

    def affine(stat, got, gain):
        both = stat[...] + got[...]
        grouped = jnp.dot(both, ones_ref[...], precision=lax.Precision.HIGHEST, preferred_element_type=f32) / members
        centre, square = grouped[:clips], grouped[clips:2 * clips]
        scale = lax.rsqrt(square - centre * centre + NORM_EPS) * gain[...]
        return scale, -centre * scale

    def act(v, scale, shift):
        h = v * (0.5 * scale) + 0.5 * shift
        return h + h * jnp.tanh(h)

    send_stat1.wait()
    scale1, shift1 = affine(stat1, got1, gain1_ref)

    def spread(v, put):
        col = lax.broadcasted_iota(jnp.int32, v.shape, 0) % cols
        put(0, jnp.where(col == 0, 0.0, pltpu.roll(v, 1, 0)).astype(bf16))
        put(1, v.astype(bf16))
        put(2, jnp.where(col == cols - 1, 0.0, pltpu.roll(v, v.shape[0] - 1, 0)).astype(bf16))

    lines = block // cols
    for c in range(clips):
        for t in range(frames):
            def fill(i, carry, c=c, t=t):
                r = i * lines
                v = vid[c, t, pl.ds(r, lines)].reshape(block, ch).astype(f32)
                v = act(v, scale1[c:c + 1], shift1[c:c + 1])

                def put(e, w):
                    wide[c, t, pl.ds(r + 1, lines), :, e * ch:(e + 1) * ch] = w.reshape(lines, cols, ch)

                spread(v, put)
                return carry

            lax.fori_loop(0, rows // lines, fill, 0)

    send_halo.wait()
    near = (rows + 1) * (1 - strip)
    far = (rows + 1) * strip
    for c in range(clips):
        for t in range(frames):
            v = act(halo[c, t].reshape(cols, ch).astype(f32), scale1[c:c + 1], shift1[c:c + 1])

            def put(e, w, c=c, t=t):
                wide[c, t, pl.ds(near, 1), :, e * ch:(e + 1) * ch] = w.reshape(1, cols, ch)

            spread(v, put)
            wide[c, t, pl.ds(far, 1)] = jnp.zeros((1, cols, 3 * ch), bf16)

    send_count.wait()
    count_chip[...] = count_own[...] + count_core[...]
    plane_counts = [
        remote(count_chip, count_plane.at[i], cp_send.at[i], cp_recv.at[i], peer) for i, peer in enumerate(plane_peers)
    ]
    for copy in plane_counts:
        copy.start()

    for copy in load_weight:
        copy.wait()
    last = taps - 1
    for c in range(clips):
        total = None
        for a in range(taps):
            have = frames - (last - a)
            left = jnp.concatenate(
                [wide[c, :have, b:b + rows].reshape(have * per_frame, 3 * ch) for b in range(3)], axis=1
            )
            right = weight[a].reshape(9 * ch, ch)
            part = jnp.dot(left, right, preferred_element_type=f32)
            start = (last - a) * per_frame
            if a == 0:
                hid[c, :start] = vid[c].reshape(per_clip, ch)[:start].astype(f32)
                hid[c, start:] = vid[c].reshape(per_clip, ch)[start:].astype(f32) + part
            else:
                hid[c, start:] = hid[c, start:] + part
        first = second = jnp.zeros((8, ch), f32)

        def add(i, carry, c=c):
            v = hid[c, pl.ds(pl.multiple_of(i * block, block), block)]
            return carry[0] + fold(v), carry[1] + fold(v * v)

        first, second = lax.fori_loop(0, per_clip // block, add, (first, second), unroll=True)
        stat2[pl.ds(c, 1)] = first.sum(axis=0, keepdims=True)
        stat2[pl.ds(clips + c, 1)] = second.sum(axis=0, keepdims=True)

    send_stat2 = remote(stat2, got2, part_send.at[2], part_recv.at[2], partner)
    send_stat2.start()

    total = count_chip[...]
    for i, copy in enumerate(plane_counts):
        copy.wait()
        total = total + count_plane[i]
    count_z[z] = total
    z_counts = [
        remote(count_z.at[z], count_z.at[z], cz_send.at[i], cz_recv.at[i], peer) for i, peer in enumerate(z_peers)
    ]
    for copy in z_counts:
        copy.start()
    load_sums.wait()
    old = ema_count_ref[...]
    n_old = jnp.sum(old)
    smooth = (old + SMOOTH_EPS) / (n_old + CODES * SMOOTH_EPS) * n_old
    for j in range(CODES // span):
        down = jnp.broadcast_to(smooth[:, j * span:(j + 1) * span], (span, span)).T
        entry = ema_sum[j * span:(j + 1) * span] / jnp.concatenate([down] * (EMB // span), axis=1)
        high = entry.astype(bf16)
        book[j * span:(j + 1) * span, :EMB] = high
        book[j * span:(j + 1) * span, EMB:] = (entry - high.astype(f32)).astype(bf16)

    send_stat2.wait()
    scale2, shift2 = affine(stat2, got2, gain2_ref)
    for c in range(clips):
        def second_act(i, carry, c=c):
            r = pl.multiple_of(i * block, block)
            act2[pl.ds(c * per_clip + r, block)] = act(
                hid[c, pl.ds(r, block)], scale2[c:c + 1], shift2[c:c + 1]
            ).astype(bf16)
            return carry

        lax.fori_loop(0, per_clip // block, second_act, 0)

    write_act = pltpu.make_async_copy(act2, act_hbm, load_sem.at[clips + taps + 1])
    write_act.start()

    def sums_of(start):
        mine = jnp.dot(member[pl.ds(start, HALF)], act2[...], preferred_element_type=f32)
        high = mine.astype(bf16)
        low = (mine - high.astype(f32)).astype(bf16)
        return jnp.dot(high, proj_ref[...], preferred_element_type=f32) + jnp.dot(
            low, proj_ref[...], preferred_element_type=f32
        )

    core_out[...] = sums_of(pl.multiple_of((1 - core) * HALF, HALF)).astype(bf16)
    send_core = remote(core_out, core_in, core_sem.at[2], core_sem.at[3], other_core)
    send_core.start()
    lat[:HALF] = sums_of(pl.multiple_of(core * HALF, HALF))
    send_core.wait()
    half_rows = lat[:HALF] + core_in[...].astype(f32)
    lat[:HALF] = half_rows
    half[...] = half_rows.astype(bf16)

    scatter = [
        remote(
            half.at[pl.ds(pl.multiple_of(plane_chunks[i] * CHUNK, CHUNK), CHUNK)],
            plane_in.at[i], rs_send.at[i], rs_recv.at[i], peer,
        )
        for i, peer in enumerate(plane_peers)
    ]
    for copy in scatter:
        copy.start()
    total = lat[pl.ds(pl.multiple_of(own_chunk * CHUNK, CHUNK), CHUNK)]
    for i, copy in enumerate(scatter):
        copy.wait()
        total = total + plane_in[i].astype(f32)

    z_buf[z] = total.astype(bf16)
    along = [remote(z_buf.at[z], z_buf.at[z], z_send.at[i], z_recv.at[i], peer) for i, peer in enumerate(z_peers)]
    for copy in along:
        copy.start()

    for c in range(clips):
        part = jnp.zeros((8, EMB), f32)
        for j in range(per_clip // 256):
            at = c * per_clip + j * 256
            picked = lax.dot_general(
                member[:, at:at + 256], book[...], (((0,), (0,)), ((), ())), preferred_element_type=f32
            )
            value = jnp.dot(act2[at:at + 256], proj_ref[...], preferred_element_type=f32)
            gap = value - (picked[:, :EMB] + picked[:, EMB:])
            part += fold(gap * gap)
        errs[pl.ds(c, 1)] = part.sum(axis=0, keepdims=True)
    send_err = remote(errs, got_err, part_send.at[3], part_recv.at[3], partner)
    send_err.start()

    for copy in along:
        copy.wait()
    total = z_buf[0].astype(f32)
    for i in range(1, Z):
        total = total + z_buf[i].astype(f32)
    base = core * HALF
    own_rows = pl.ds(pl.multiple_of(base + own_chunk * CHUNK, CHUNK), CHUNK)
    sums_ref[own_rows] = total.astype(bf16)
    gather = [
        remote(sums_ref.at[own_rows], sums_ref.at[own_rows], ag_send.at[i], ag_recv.at[i], peer)
        for i, peer in enumerate(plane_peers)
    ]
    for copy in gather:
        copy.start()
    forward = [remote(sums_ref.at[own_rows], sums_ref.at[own_rows], fw_send.at[PLANE - 1], fw_recv.at[PLANE - 1], other_core)]
    forward[0].start()
    for i in reversed(range(PLANE - 1)):
        gather[i].wait_recv()
        here = pl.ds(pl.multiple_of(base + from_chunks[i] * CHUNK, CHUNK), CHUNK)
        copy = remote(sums_ref.at[here], sums_ref.at[here], fw_send.at[i], fw_recv.at[i], other_core)
        copy.start()
        forward.append(copy)

    for copy in z_counts:
        copy.wait()
    total = count_z[0]
    for i in range(1, Z):
        total = total + count_z[i]
    counts_ref[...] = total
    send_err.wait()
    err = (errs[...] + got_err[...]).sum(axis=1, keepdims=True) / (2 * per_clip * EMB)
    err_ref[...] = jnp.broadcast_to(err, err_ref.shape)

    for copy in gather:
        copy.wait_send()
    for copy in forward:
        copy.wait()
    write_act.wait()


def smoothed_book(sums, counts, grand):
    smooth = (counts + SMOOTH_EPS) / (grand + CODES * SMOOTH_EPS) * grand
    return sums / smooth[:, None]


def body(video, gain_first, conv_weight, gain_second, proj_weight, codes, ema_sum, ema_count):
    clips, frames, rows, cols, ch = video.shape
    tokens = clips * frames * rows * cols
    taps = min(frames, conv_weight.shape[0])
    group = ch // GROUPS
    number = jnp.arange(ch) // group
    ones = (number[:, None] == number[None, :]).astype(f32)
    vmem = pl.BlockSpec(memory_space=pltpu.VMEM)
    hbm = pl.BlockSpec(memory_space=pl.ANY)
    near = PLANE - 1
    dma = pltpu.SemaphoreType.DMA
    act2, sums, counts, err = pl.pallas_call(
        kernel,
        out_shape=(
            jax.ShapeDtypeStruct((tokens, ch), bf16),
            jax.ShapeDtypeStruct((CODES, EMB), bf16),
            jax.ShapeDtypeStruct((1, CODES), f32),
            jax.ShapeDtypeStruct((8, 128), f32),
        ),
        in_specs=[hbm, hbm, vmem, vmem, vmem, vmem, hbm, vmem, vmem],
        out_specs=(hbm, vmem, vmem, vmem),
        scratch_shapes=[
            pltpu.VMEM(video.shape, bf16),
            pltpu.VMEM((clips, frames, 1, cols, ch), bf16),
            pltpu.VMEM((taps,) + conv_weight.shape[1:], bf16),
            pltpu.VMEM((clips, frames, rows + 2, cols, 3 * ch), bf16),
            pltpu.VMEM((clips, frames * rows * cols, ch), f32),
            pltpu.VMEM((tokens, ch), bf16),
            pltpu.VMEM((CODES, tokens), bf16),
            pltpu.VMEM((CODES, 2 * EMB), bf16),
            pltpu.VMEM((CODES, EMB), f32),
            pltpu.VMEM((HALF, EMB), f32),
            pltpu.VMEM((8, ch), f32),
            pltpu.VMEM((8, ch), f32),
            pltpu.VMEM((8, ch), f32),
            pltpu.VMEM((8, ch), f32),
            pltpu.VMEM((8, EMB), f32),
            pltpu.VMEM((8, EMB), f32),
            pltpu.VMEM((1, CODES), f32),
            pltpu.VMEM((1, CODES), f32),
            pltpu.VMEM((1, CODES), f32),
            pltpu.VMEM((near, 1, CODES), f32),
            pltpu.VMEM((Z, 1, CODES), f32),
            pltpu.VMEM((HALF, EMB), bf16),
            pltpu.VMEM((HALF, EMB), bf16),
            pltpu.VMEM((HALF, EMB), bf16),
            pltpu.VMEM((near, CHUNK, EMB), bf16),
            pltpu.VMEM((Z, CHUNK, EMB), bf16),
            dma((clips + taps + 2,)),
            dma((4,)), dma((4,)), dma((4,)),
            dma((near,)), dma((near,)), dma((Z - 1,)), dma((Z - 1,)),
            dma((near,)), dma((near,)), dma((PLANE,)), dma((PLANE,)),
            dma((near,)), dma((near,)), dma((Z - 1,)), dma((Z - 1,)),
        ],
        compiler_params=pltpu.CompilerParams(collective_id=0, has_side_effects=True),
    )(
        video, conv_weight, gain_first.reshape(1, -1), gain_second.reshape(1, -1), proj_weight,
        codes.reshape(1, -1), ema_sum, ema_count.reshape(1, -1), ones,
    )
    latent = jnp.dot(act2, proj_weight, preferred_element_type=f32)
    code_count = DECAY * ema_count + (1.0 - DECAY) * counts[0]
    codebook = smoothed_book(
        DECAY * ema_sum + (1.0 - DECAY) * sums.astype(f32), code_count, jnp.sum(code_count)
    )
    return (latent.reshape(video.shape[:4] + (EMB,)), codebook, code_count, err[:clips, 0])


def solution(mesh):
    tiles = P("clip", None, "strip", None, None)
    in_specs = (tiles, P(), P(), P(), P(), P("clip", None, "strip", None), P(), P())
    out_specs = (tiles, P(), P(), P("clip"))
    return jax.shard_map(body, mesh=mesh, in_specs=in_specs, out_specs=out_specs, check_vma=False)
```

```python
import jax
import jax.numpy as jnp
from jax import lax
from jax.experimental import pallas as pl
from jax.experimental.pallas import tpu as pltpu
from jax.sharding import PartitionSpec as P

EMB = 256
CODES = 1024
GROUPS = 32
NORM_EPS = 1e-06
SMOOTH_EPS = 1e-05
DECAY = 0.9
MESH = pl.DeviceIdType.MESH

X, Y, Z, CORES = 4, 4, 8, 2
PLANE = X * Y
HALF = CODES // CORES
WAVES = 2
WAVE = HALF // WAVES
CHUNK = WAVE // PLANE
NEAR = PLANE - 1
SPAN = 128
bf16, f32 = jnp.bfloat16, jnp.float32


def address(x, y, z, core):
    return (((y // 2 * X + x) * Z + z) * CORES + core, y % 2)


def shifts():
    every = [(dx, dy) for dx in range(X) for dy in range(Y) if dx or dy]
    return sorted(every, key=lambda s: -(min(s[0], X - s[0]) + min(s[1], Y - s[1])))


def z_shifts():
    return sorted(range(1, Z), key=lambda d: -min(d, Z - d))


def ds(start, size):
    return pl.ds(pl.multiple_of(start, size), size)


def fold(v):
    return v.reshape(v.shape[0] // 8, 8, v.shape[1]).sum(axis=0)


def down(row):
    return jnp.broadcast_to(row, (SPAN, SPAN)).T


def smoothed(counts):
    grand = jnp.sum(counts)
    return (counts + SMOOTH_EPS) / (grand + CODES * SMOOTH_EPS) * grand


def kernel(
    video_hbm, weight_hbm, gain1_hbm, gain2_hbm, proj_hbm, codes_hbm, ema_sum_hbm, ema_count_hbm,
    act_hbm, sums_ref, counts_ref, err_ref,
    vid, halo, weight, wide, hid, act2, member, book, ema_sum, raw, codes_in, codes_at,
    gain1_ref, gain2_ref, proj_ref, ema_count_ref,
    stat1, stat2, got1, got2, errs, got_err,
    count_own, count_core, count_chip, count_plane, count_z,
    core_out, core_in, half, plane_in, z_buf,
    load_sem, part_send, part_recv, cc_sem, core_send, core_recv,
    rs_send, rs_recv, z_send, z_recv, ag_send, ag_recv, fw_send, fw_recv,
    cp_sem, cz_sem,
):
    clips, frames, rows, cols, ch = vid.shape
    per_frame = rows * cols
    per_clip = frames * per_frame
    taps = weight.shape[0]
    skip = weight_hbm.shape[0] - taps

    def load(src, dst, i):
        copy = pltpu.make_async_copy(src, dst, load_sem.at[i])
        copy.start()
        return copy

    load_video = [load(video_hbm.at[c], vid.at[c], c) for c in range(clips)]
    load_codes = load(codes_hbm, codes_in, clips)
    load_small = [
        load(src, dst, clips + 1 + i)
        for i, (src, dst) in enumerate(
            [(gain1_hbm, gain1_ref), (gain2_hbm, gain2_ref), (ema_count_hbm, ema_count_ref), (proj_hbm, proj_ref)]
        )
    ]
    load_weight = [load(weight_hbm.at[skip + a], weight.at[a], clips + 5 + a) for a in range(taps)]

    clip, strip = lax.axis_index("clip"), lax.axis_index("strip")
    core = clip % CORES
    z = clip // CORES % Z
    x = clip // (CORES * Z) % X
    y = clip // (CORES * Z * X) * 2 + strip
    steps = shifts()
    z_steps = z_shifts()
    partner = (clip, 1 - strip)
    other_core = address(x, y, z, 1 - core)
    plane_peers = [address((x + dx) % X, (y + dy) % Y, z, core) for dx, dy in steps]
    plane_chunks = [(y + dy) % Y * X + (x + dx) % X for dx, dy in steps]
    own_chunk = y * X + x
    z_peers = [address(x, y, (z + d) % Z, core) for d in z_steps]

    barrier = pltpu.get_barrier_semaphore()
    everyone = plane_peers + z_peers + [other_core]
    for peer in everyone:
        pl.semaphore_signal(barrier, inc=1, device_id=peer, device_id_type=MESH)

    def remote(src, dst, send, recv, peer):
        return pltpu.make_async_remote_copy(
            src_ref=src, dst_ref=dst, send_sem=send, recv_sem=recv, device_id=peer, device_id_type=MESH
        )

    def push(src, dst, send, recv, peer):
        copy = remote(src, dst, send, recv, peer)
        copy.start()
        return copy

    block = 128
    lines = block // cols
    for ref in (stat1, stat2, errs):
        ref[...] = jnp.zeros_like(ref)
    for c in range(clips):
        load_video[c].wait()
        first = second = jnp.zeros((8, ch), f32)
        for t in range(frames):
            def add(i, carry, c=c, t=t):
                r = pl.multiple_of(i * lines, lines)
                v = vid[c, t, pl.ds(r, lines)].reshape(block, ch).astype(f32)
                return carry[0] + fold(v), carry[1] + fold(v * v)
            first, second = lax.fori_loop(0, per_frame // block, add, (first, second), unroll=True)
        stat1[pl.ds(c, 1)] = first.sum(axis=0, keepdims=True)
        stat1[pl.ds(clips + c, 1)] = second.sum(axis=0, keepdims=True)

    pl.semaphore_wait(barrier, len(everyone))
    send_stat1 = push(stat1, got1, part_send.at[0], part_recv.at[0], partner)
    edge = (rows - 1) * (1 - strip)
    send_halo = push(video_hbm.at[:, :, pl.ds(edge, 1)], halo, part_send.at[1], part_recv.at[1], partner)

    load_codes.wait()
    quads = rows // lines
    for c in range(clips):
        for t in range(frames):
            codes_at[pl.ds((c * frames + t) * quads, quads)] = jnp.concatenate(
                [codes_in[c, t, pl.ds(p, quads, stride=lines)] for p in range(lines)], axis=1
            )
    blocks = clips * frames * quads

    def mark(i, carry):
        k = pl.multiple_of(i * SPAN, SPAN)
        number = lax.broadcasted_iota(jnp.int32, (SPAN, block), 0) + k
        total = jnp.zeros((SPAN, block), f32)
        for j in range(blocks):
            hit = jnp.where(number == codes_at[j:j + 1], 1.0, 0.0)
            total += hit
            member[pl.ds(k, SPAN), j * block:(j + 1) * block] = hit.astype(bf16)
        lanes = jnp.broadcast_to(total.sum(axis=1, keepdims=True), (SPAN, SPAN))
        count_own[:, pl.ds(k, SPAN)] = lanes.T[:1]
        return carry

    lax.fori_loop(0, CODES // SPAN, mark, 0)
    send_count = push(count_own, count_core, cc_sem.at[0], cc_sem.at[1], other_core)

    members = per_clip * 2 * (ch // GROUPS)
    group = ch // GROUPS
    same = (
        lax.broadcasted_iota(jnp.int32, (ch, ch), 0) // group == lax.broadcasted_iota(jnp.int32, (ch, ch), 1) // group
    )
    ones = jnp.where(same, 1.0, 0.0).astype(f32)

    def affine(both, count, gain):
        grouped = jnp.dot(both, ones, precision=lax.Precision.HIGHEST, preferred_element_type=f32) / members
        centre, square = grouped[:count], grouped[count:2 * count]
        scale = lax.rsqrt(square - centre * centre + NORM_EPS) * gain[...]
        return scale, -centre * scale

    def act(v, scale, shift):
        h = v * (0.5 * scale) + 0.5 * shift
        return h + h * jnp.tanh(h)

    for copy in load_small:
        copy.wait()
    send_stat1.wait()
    scale1, shift1 = affine(stat1[...] + got1[...], clips, gain1_ref)

    def spread(v, put):
        col = lax.broadcasted_iota(jnp.int32, v.shape, 0) % cols
        put(0, jnp.where(col == 0, 0.0, pltpu.roll(v, 1, 0)).astype(bf16))
        put(1, v.astype(bf16))
        put(2, jnp.where(col == cols - 1, 0.0, pltpu.roll(v, v.shape[0] - 1, 0)).astype(bf16))

    for c in range(clips):
        for t in range(frames):
            def fill(i, carry, c=c, t=t):
                r = i * lines
                v = vid[c, t, pl.ds(r, lines)].reshape(block, ch).astype(f32)
                v = act(v, scale1[c:c + 1], shift1[c:c + 1])

                def put(e, w):
                    wide[c, t, pl.ds(r + 1, lines), :, e * ch:(e + 1) * ch] = w.reshape(lines, cols, ch)

                spread(v, put)
                return carry

            lax.fori_loop(0, rows // lines, fill, 0)

    send_halo.wait()
    near = (rows + 1) * (1 - strip)
    far = (rows + 1) * strip
    for c in range(clips):
        for t in range(frames):
            v = act(halo[c, t].reshape(cols, ch).astype(f32), scale1[c:c + 1], shift1[c:c + 1])

            def put(e, w, c=c, t=t):
                wide[c, t, pl.ds(near, 1), :, e * ch:(e + 1) * ch] = w.reshape(1, cols, ch)

            spread(v, put)
            wide[c, t, pl.ds(far, 1)] = jnp.zeros((1, cols, 3 * ch), bf16)

    send_count.wait()
    count_chip[...] = count_own[...] + count_core[...]
    plane_counts = [
        push(count_chip, count_plane.at[i], cp_sem.at[0], cp_sem.at[1], peer) for i, peer in enumerate(plane_peers)
    ]

    for copy in load_weight:
        copy.wait()
    load_sums = load(ema_sum_hbm, ema_sum, clips + 5 + taps)
    last = taps - 1
    send_stat2 = []
    for c in range(clips):
        for a in range(taps):
            have = frames - (last - a)
            left = jnp.concatenate(
                [wide[c, :have, b:b + rows].reshape(have * per_frame, 3 * ch) for b in range(3)], axis=1
            )
            right = weight[a].reshape(9 * ch, ch)
            part = jnp.dot(left, right, preferred_element_type=f32)
            start = (last - a) * per_frame
            if a == 0:
                hid[c, :start] = vid[c].reshape(per_clip, ch)[:start].astype(f32)
                hid[c, start:] = vid[c].reshape(per_clip, ch)[start:].astype(f32) + part
            else:
                hid[c, start:] = hid[c, start:] + part

        def add(i, carry, c=c):
            v = hid[c, ds(i * block, block)]
            return carry[0] + fold(v), carry[1] + fold(v * v)

        zero = jnp.zeros((8, ch), f32)
        first, second = lax.fori_loop(0, per_clip // block, add, (zero, zero), unroll=True)
        stat2[c, 0:1] = first.sum(axis=0, keepdims=True)
        stat2[c, 1:2] = second.sum(axis=0, keepdims=True)
        send_stat2.append(push(stat2.at[c], got2.at[c], part_send.at[2 + c], part_recv.at[2 + c], partner))

    every_count = remote(count_plane, count_plane, cp_sem.at[0], cp_sem.at[1], partner)
    every_count.wait()
    total = count_chip[...]
    for i in range(NEAR):
        total = total + count_plane[i]
    count_z[z] = total
    for peer in z_peers:
        push(count_z.at[z], count_z.at[z], cz_sem.at[0], cz_sem.at[1], peer)

    far_half, own_half = ds((1 - core) * HALF, HALF), ds(core * HALF, HALF)
    for c in range(clips):
        send_stat2[c].wait()
        scale2, shift2 = affine(stat2[c] + got2[c], 1, gain2_ref)

        def second_act(i, carry, c=c):
            r = pl.multiple_of(i * block, block)
            act2[pl.ds(c * per_clip + r, block)] = act(hid[c, pl.ds(r, block)], scale2, shift2).astype(bf16)
            return carry

        lax.fori_loop(0, per_clip // block, second_act, 0)
        if c < clips - 1:
            mine = act2[c * per_clip:(c + 1) * per_clip]
            for i, place in enumerate((far_half, own_half)):
                part = jnp.dot(
                    member[place, c * per_clip:(c + 1) * per_clip], mine, preferred_element_type=f32
                )
                raw[i] = part if c == 0 else raw[i] + part

    write_act = load(act2, act_hbm, clips + 6 + taps)

    def sums_of(i, w):
        start = ((1 - core) if i == 0 else core) * HALF + w * WAVE
        c = clips - 1
        mine = raw[i, w * WAVE:(w + 1) * WAVE] + jnp.dot(
            member[ds(start, WAVE), c * per_clip:(c + 1) * per_clip],
            act2[c * per_clip:(c + 1) * per_clip], preferred_element_type=f32,
        )
        high = mine.astype(bf16)
        low = (mine - high.astype(f32)).astype(bf16)
        return jnp.dot(high, proj_ref[...], preferred_element_type=f32) + jnp.dot(
            low, proj_ref[...], preferred_element_type=f32
        )

    send_core = []
    for w in range(WAVES):
        core_out[w] = sums_of(0, w).astype(bf16)
        send_core.append(push(core_out.at[w], core_in.at[w], core_send.at[w], core_recv.at[w], other_core))
    for w in range(WAVES):
        own = sums_of(1, w)
        send_core[w].wait()
        own = own + core_in[w].astype(f32)
        raw[1, w * WAVE:(w + 1) * WAVE] = own
        half[w] = own.astype(bf16)
        for i, peer in enumerate(plane_peers):
            push(half.at[w, ds(plane_chunks[i] * CHUNK, CHUNK)], plane_in.at[w, i], rs_send.at[w], rs_recv.at[w], peer)

    for w in range(WAVES):
        remote(plane_in.at[w], plane_in.at[w], rs_send.at[w], rs_recv.at[w], partner).wait()
        total = raw[1, ds(w * WAVE + own_chunk * CHUNK, CHUNK)]
        for i in range(NEAR):
            total = total + plane_in[w, i].astype(f32)
        z_buf[w, z] = total.astype(bf16)
        for peer in z_peers:
            push(z_buf.at[w, z], z_buf.at[w, z], z_send.at[w], z_recv.at[w], peer)

    load_sums.wait()
    smooth = smoothed(ema_count_ref[...])
    for j in range(CODES // SPAN):
        scale = jnp.concatenate([down(smooth[:, j * SPAN:(j + 1) * SPAN])] * (EMB // SPAN), axis=1)
        entry = ema_sum[j * SPAN:(j + 1) * SPAN] / scale
        high = entry.astype(bf16)
        book[j * SPAN:(j + 1) * SPAN, :EMB] = high
        book[j * SPAN:(j + 1) * SPAN, EMB:] = (entry - high.astype(f32)).astype(bf16)

    def distances(c):
        part = jnp.zeros((8, EMB), f32)
        for j in range(per_clip // 256):
            at = c * per_clip + j * 256
            picked = lax.dot_general(
                member[:, at:at + 256], book[...], (((0,), (0,)), ((), ())), preferred_element_type=f32
            )
            value = jnp.dot(act2[at:at + 256], proj_ref[...], preferred_element_type=f32)
            gap = value - (picked[:, :EMB] + picked[:, EMB:])
            part += fold(gap * gap)
        errs[pl.ds(c, 1)] = part.sum(axis=0, keepdims=True)

    for c in range(clips):
        distances(c)
    send_err = push(errs, got_err, part_send.at[2 + clips], part_recv.at[2 + clips], partner)

    base = core * HALF
    for w in range(WAVES):
        arrived = z_buf.at[w, pl.ds(0, Z - 1)]
        remote(arrived, arrived, z_send.at[w], z_recv.at[w], partner).wait()
        total = z_buf[w, 0].astype(f32)
        for i in range(1, Z):
            total = total + z_buf[w, i].astype(f32)
        own_rows = ds(base + w * WAVE + own_chunk * CHUNK, CHUNK)
        sums_ref[own_rows] = total.astype(bf16)
        for peer in plane_peers:
            push(sums_ref.at[own_rows], sums_ref.at[own_rows], ag_send.at[w], ag_recv.at[w], peer)

    arrived = count_z.at[pl.ds(0, Z - 1)]
    remote(arrived, arrived, cz_sem.at[0], cz_sem.at[1], partner).wait()
    total = count_z[0]
    for i in range(1, Z):
        total = total + count_z[i]
    counts_ref[...] = total
    send_err.wait()
    err = (errs[...] + got_err[...]).sum(axis=1, keepdims=True) / (2 * per_clip * EMB)
    err_ref[...] = jnp.broadcast_to(err, err_ref.shape)

    forward = []
    for w in range(WAVES):
        remote(plane_in.at[w], plane_in.at[w], ag_send.at[w], ag_recv.at[w], partner).wait()
        here = ds(base + w * WAVE, WAVE)
        forward.append(push(sums_ref.at[here], sums_ref.at[here], fw_send.at[w], fw_recv.at[w], other_core))
    for copy in forward:
        copy.wait()
    write_act.wait()


def finish(
    act_hbm, sums_hbm, counts_hbm, ema_sum_hbm, ema_count_hbm, proj_hbm, err_hbm,
    latent_hbm, book_hbm, count_ref, err_out,
    act2, sums, counts, ema_sum, ema_count, proj, err, latent, book, in_sem, out_sem,
):
    tokens = act2.shape[0]
    parts = 4
    step = tokens // parts
    turn = CODES // parts

    def load(src, dst, i):
        copy = pltpu.make_async_copy(src, dst, in_sem.at[i])
        copy.start()
        return copy

    small = [
        load(src, dst, i)
        for i, (src, dst) in enumerate(
            [(proj_hbm, proj), (counts_hbm, counts), (ema_count_hbm, ema_count), (err_hbm, err)]
        )
    ]
    acts = [load(act_hbm.at[pl.ds(i * step, step)], act2.at[pl.ds(i * step, step)], 4 + i) for i in range(parts)]
    terms = [load(sums_hbm, sums, 4 + parts), load(ema_sum_hbm, ema_sum, 5 + parts)]
    for copy in small:
        copy.wait()
    out = []

    def put(src, dst):
        copy = pltpu.make_async_copy(src, dst, out_sem.at[len(out)])
        copy.start()
        out.append(copy)

    for i in range(parts):
        acts[i].wait()
        at = pl.ds(i * step, step)
        latent[at] = jnp.dot(act2[at], proj[...], preferred_element_type=f32)
        put(latent.at[at], latent_hbm.at[at])
    code_count = DECAY * ema_count[...] + (1.0 - DECAY) * counts[...]
    count_ref[...] = code_count
    smooth = smoothed(code_count)
    for i in range(err_out.shape[0]):
        err_out[i] = err[i, 0]
    for copy in terms:
        copy.wait()
    for i in range(parts):
        for j in range(i * turn // SPAN, (i + 1) * turn // SPAN):
            at = pl.ds(j * SPAN, SPAN)
            scale = jnp.concatenate([down(smooth[:, j * SPAN:(j + 1) * SPAN])] * (EMB // SPAN), axis=1)
            book[at] = (DECAY * ema_sum[at] + (1.0 - DECAY) * sums[at].astype(f32)) / scale
        at = pl.ds(i * turn, turn)
        put(book.at[at], book_hbm.at[at])
    for copy in out:
        copy.wait()


def body(video, gain_first, conv_weight, gain_second, proj_weight, codes, ema_sum, ema_count):
    clips, frames, rows, cols, ch = video.shape
    tokens = clips * frames * rows * cols
    taps = min(frames, conv_weight.shape[0])
    vmem = pl.BlockSpec(memory_space=pltpu.VMEM)
    near = pl.BlockSpec(memory_space=pl.ANY)
    hbm = pl.BlockSpec(memory_space=pltpu.HBM)
    dma = pltpu.SemaphoreType.DMA
    V = pltpu.VMEM
    count_row = ema_count.reshape(1, -1)
    keep = lambda a: pltpu.with_memory_space_constraint(a, pltpu.HBM)
    video, conv_weight, proj_weight, codes, ema_sum, count_row = map(keep, (video, conv_weight, proj_weight, codes, ema_sum, count_row))
    gain_first, gain_second = keep(gain_first.reshape(1,-1)), keep(gain_second.reshape(1,-1))
    act2, sums, counts, err = pl.pallas_call(
        kernel,
        out_shape=(
            jax.ShapeDtypeStruct((tokens, ch), bf16),
            jax.ShapeDtypeStruct((CODES, EMB), bf16),
            jax.ShapeDtypeStruct((1, CODES), f32),
            jax.ShapeDtypeStruct((8, 128), f32),
        ),
        in_specs=[hbm] * 8,
        out_specs=(near, vmem, vmem, vmem),
        scratch_shapes=[
            V(video.shape, bf16),
            V((clips, frames, 1, cols, ch), bf16),
            V((taps,) + conv_weight.shape[1:], bf16),
            V((clips, frames, rows + 2, cols, 3 * ch), bf16),
            V((clips, frames * rows * cols, ch), f32),
            V((tokens, ch), bf16),
            V((CODES, tokens), bf16),
            V((CODES, 2 * EMB), bf16),
            V((CODES, EMB), f32),
            V((2, HALF, EMB), f32),
            V(codes.shape, jnp.int32),
            V((tokens // 128, 128), jnp.int32),
            V((1, ch), f32), V((1, ch), f32), V(proj_weight.shape, bf16), V((1, CODES), f32),
            V((8, ch), f32), V((clips, 8, ch), f32), V((8, ch), f32), V((clips, 8, ch), f32),
            V((8, EMB), f32), V((8, EMB), f32),
            V((1, CODES), f32), V((1, CODES), f32), V((1, CODES), f32),
            V((NEAR, 1, CODES), f32), V((Z, 1, CODES), f32),
            V((WAVES, WAVE, EMB), bf16), V((WAVES, WAVE, EMB), bf16), V((WAVES, WAVE, EMB), bf16),
            V((WAVES, NEAR, CHUNK, EMB), bf16), V((WAVES, Z, CHUNK, EMB), bf16),
            dma((clips + taps + 7,)),
            dma((clips + 3,)), dma((clips + 3,)), dma((2,)),
        ] + [dma((WAVES,))] * 10 + [dma((2,))] * 2,
        compiler_params=pltpu.CompilerParams(
            collective_id=0, has_side_effects=True, vmem_limit_bytes=32 << 20
        ),
    )(
        video, conv_weight, gain_first.reshape(1, -1), gain_second.reshape(1, -1), proj_weight,
        codes, ema_sum, count_row,
    )
    latent, codebook, code_count, clip_error = pl.pallas_call(
        finish,
        out_shape=(
            jax.ShapeDtypeStruct((tokens, EMB), f32),
            jax.ShapeDtypeStruct((CODES, EMB), f32),
            jax.ShapeDtypeStruct((1, CODES), f32),
            jax.ShapeDtypeStruct((clips,), f32),
        ),
        in_specs=[near, near, near, hbm, hbm, hbm, near],
        out_specs=(hbm, hbm, vmem, pl.BlockSpec(memory_space=pltpu.SMEM)),
        scratch_shapes=[
            V((tokens, ch), bf16), V((CODES, EMB), bf16), V((1, CODES), f32), V((CODES, EMB), f32),
            V((1, CODES), f32), V(proj_weight.shape, bf16), V((8, 128), f32),
            V((tokens, EMB), f32), V((CODES, EMB), f32), dma((10,)), dma((8,)),
        ],
        compiler_params=pltpu.CompilerParams(vmem_limit_bytes=16 << 20),
    )(act2, sums, counts, ema_sum, count_row, proj_weight, err)
    return (latent.reshape(video.shape[:4] + (EMB,)), codebook, code_count.reshape(-1), clip_error)


def solution(mesh):
    tiles = P("clip", None, "strip", None, None)
    in_specs = (tiles, P(), P(), P(), P(), P("clip", None, "strip", None), P(), P())
    out_specs = (tiles, P(), P(), P("clip"))
    return jax.shard_map(body, mesh=mesh, in_specs=in_specs, out_specs=out_specs, check_vma=False)
```

```python
import jax
import jax.numpy as jnp
from jax import lax
from jax.experimental import pallas as pl
from jax.experimental.pallas import tpu as pltpu
from jax.sharding import PartitionSpec as P

EMB = 256
CODES = 1024
GROUPS = 32
NORM_EPS = 1e-06
SMOOTH_EPS = 1e-05
DECAY = 0.9
MESH = pl.DeviceIdType.MESH

X, Y, Z, CORES = 4, 4, 8, 2
PLANE = X * Y
HALF = CODES // CORES
WAVES = 2
WAVE = HALF // WAVES
CHUNK = WAVE // PLANE
NEAR = PLANE - 1
SPAN = 128
PIECES = 2
bf16, f32 = jnp.bfloat16, jnp.float32


def address(x, y, z, core):
    return (((y // 2 * X + x) * Z + z) * CORES + core, y % 2)


def shifts():
    every = [(dx, dy) for dx in range(X) for dy in range(Y) if dx or dy]
    return sorted(every, key=lambda s: -(min(s[0], X - s[0]) + min(s[1], Y - s[1])))


def z_shifts():
    return sorted(range(1, Z), key=lambda d: -min(d, Z - d))


def ds(start, size):
    return pl.ds(pl.multiple_of(start, size), size)


def fold(v):
    return v.reshape(v.shape[0] // 8, 8, v.shape[1]).sum(axis=0)


def down(row):
    return jnp.broadcast_to(row, (SPAN, SPAN)).T


def smoothed(counts):
    grand = jnp.sum(counts)
    return (counts + SMOOTH_EPS) / (grand + CODES * SMOOTH_EPS) * grand


def kernel(
    video_hbm, weight_hbm, gain1_hbm, gain2_hbm, proj_hbm, codes_hbm, ema_sum_hbm, ema_count_hbm,
    latent, ema_sum, sums_ref, counts_ref, err_ref,
    vid, halo, weight, wide, hid, act2, member, book, raw, codes_in, codes_at,
    gain1_ref, gain2_ref, proj_ref, ema_count_ref,
    stat1, stat2, got1, got2, errs, got_err,
    count_own, count_core, count_chip, count_plane, count_z,
    core_out, core_in, half, plane_in, z_buf,
    load_sem, part_send, part_recv, cc_sem, core_send, core_recv,
    rs_send, rs_recv, z_send, z_recv, ag_send, ag_recv, fw_send, fw_recv,
    cp_sem, cz_sem,
):
    clips, frames, rows, cols, ch = vid.shape
    per_frame = rows * cols
    per_clip = frames * per_frame
    taps = weight.shape[0]
    skip = weight_hbm.shape[0] - taps

    def load(src, dst, i):
        copy = pltpu.make_async_copy(src, dst, load_sem.at[i])
        copy.start()
        return copy

    load_video = [load(video_hbm.at[c], vid.at[c], c) for c in range(clips)]
    load_codes = load(codes_hbm, codes_in, clips)
    load_small = [
        load(src, dst, clips + 1 + i)
        for i, (src, dst) in enumerate(
            [(gain1_hbm, gain1_ref), (gain2_hbm, gain2_ref), (ema_count_hbm, ema_count_ref), (proj_hbm, proj_ref)]
        )
    ]
    load_weight = [load(weight_hbm.at[skip + a], weight.at[a], clips + 5 + a) for a in range(taps)]

    clip, strip = lax.axis_index("clip"), lax.axis_index("strip")
    core = clip % CORES
    z = clip // CORES % Z
    x = clip // (CORES * Z) % X
    y = clip // (CORES * Z * X) * 2 + strip
    steps = shifts()
    z_steps = z_shifts()
    partner = (clip, 1 - strip)
    other_core = address(x, y, z, 1 - core)
    plane_peers = [address((x + dx) % X, (y + dy) % Y, z, core) for dx, dy in steps]
    plane_chunks = [(y + dy) % Y * X + (x + dx) % X for dx, dy in steps]
    own_chunk = y * X + x
    z_peers = [address(x, y, (z + d) % Z, core) for d in z_steps]

    barrier = pltpu.get_barrier_semaphore()
    everyone = plane_peers + z_peers + [other_core]
    for peer in everyone:
        pl.semaphore_signal(barrier, inc=1, device_id=peer, device_id_type=MESH)

    def remote(src, dst, send, recv, peer):
        return pltpu.make_async_remote_copy(
            src_ref=src, dst_ref=dst, send_sem=send, recv_sem=recv, device_id=peer, device_id_type=MESH
        )

    def push(src, dst, send, recv, peer):
        copy = remote(src, dst, send, recv, peer)
        copy.start()
        return copy

    block = 128
    lines = block // cols
    for ref in (stat1, stat2, errs):
        ref[...] = jnp.zeros_like(ref)
    for c in range(clips):
        load_video[c].wait()
        first = second = jnp.zeros((8, ch), f32)
        for t in range(frames):
            def add(i, carry, c=c, t=t):
                r = pl.multiple_of(i * lines, lines)
                v = vid[c, t, pl.ds(r, lines)].reshape(block, ch).astype(f32)
                return carry[0] + fold(v), carry[1] + fold(v * v)
            first, second = lax.fori_loop(0, per_frame // block, add, (first, second), unroll=True)
        stat1[pl.ds(c, 1)] = first.sum(axis=0, keepdims=True)
        stat1[pl.ds(clips + c, 1)] = second.sum(axis=0, keepdims=True)

    pl.semaphore_wait(barrier, len(everyone))
    send_stat1 = push(stat1, got1, part_send.at[0], part_recv.at[0], partner)
    edge = (rows - 1) * (1 - strip)
    send_halo = push(video_hbm.at[:, :, pl.ds(edge, 1)], halo, part_send.at[1], part_recv.at[1], partner)

    load_codes.wait()
    quads = rows // lines
    for c in range(clips):
        for t in range(frames):
            codes_at[pl.ds((c * frames + t) * quads, quads)] = jnp.concatenate(
                [codes_in[c, t, pl.ds(p, quads, stride=lines)] for p in range(lines)], axis=1
            )
    def mark(c):
        first, end = c * frames * quads, (c + 1) * frames * quads

        def some(i, carry):
            k = pl.multiple_of(i * SPAN, SPAN)
            number = lax.broadcasted_iota(jnp.int32, (SPAN, block), 0) + k
            total = jnp.zeros((SPAN, block), f32)
            for j in range(first, end):
                hit = jnp.where(number == codes_at[j:j + 1], 1.0, 0.0)
                total += hit
                member[pl.ds(k, SPAN), j * block:(j + 1) * block] = hit.astype(bf16)
            found = jnp.broadcast_to(total.sum(axis=1, keepdims=True), (SPAN, SPAN)).T[:1]
            count_own[:, pl.ds(k, SPAN)] = found if c == 0 else count_own[:, pl.ds(k, SPAN)] + found
            return carry

        lax.fori_loop(0, CODES // SPAN, some, 0)

    mark(0)

    members = per_clip * 2 * (ch // GROUPS)
    group = ch // GROUPS
    same = (
        lax.broadcasted_iota(jnp.int32, (ch, ch), 0) // group == lax.broadcasted_iota(jnp.int32, (ch, ch), 1) // group
    )
    ones = jnp.where(same, 1.0, 0.0).astype(f32)

    def affine(both, count, gain):
        grouped = jnp.dot(both, ones, precision=lax.Precision.HIGHEST, preferred_element_type=f32) / members
        centre, square = grouped[:count], grouped[count:2 * count]
        scale = lax.rsqrt(square - centre * centre + NORM_EPS) * gain[...]
        return scale, -centre * scale

    def act(v, scale, shift):
        h = v * (0.5 * scale) + 0.5 * shift
        return h + h * jnp.tanh(h)

    for copy in load_small:
        copy.wait()
    send_stat1.wait()
    scale1, shift1 = affine(stat1[...] + got1[...], clips, gain1_ref)

    def spread(v, put):
        col = lax.broadcasted_iota(jnp.int32, v.shape, 0) % cols
        put(0, jnp.where(col == 0, 0.0, pltpu.roll(v, 1, 0)).astype(bf16))
        put(1, v.astype(bf16))
        put(2, jnp.where(col == cols - 1, 0.0, pltpu.roll(v, v.shape[0] - 1, 0)).astype(bf16))

    for c in range(clips):
        for t in range(frames):
            def fill(i, carry, c=c, t=t):
                r = i * lines
                v = vid[c, t, pl.ds(r, lines)].reshape(block, ch).astype(f32)
                v = act(v, scale1[c:c + 1], shift1[c:c + 1])

                def put(e, w):
                    wide[c, t, pl.ds(r + 1, lines), :, e * ch:(e + 1) * ch] = w.reshape(lines, cols, ch)

                spread(v, put)
                return carry

            lax.fori_loop(0, rows // lines, fill, 0)

    send_halo.wait()
    near = (rows + 1) * (1 - strip)
    far = (rows + 1) * strip
    for c in range(clips):
        for t in range(frames):
            v = act(halo[c, t].reshape(cols, ch).astype(f32), scale1[c:c + 1], shift1[c:c + 1])

            def put(e, w, c=c, t=t):
                wide[c, t, pl.ds(near, 1), :, e * ch:(e + 1) * ch] = w.reshape(1, cols, ch)

            spread(v, put)
            wide[c, t, pl.ds(far, 1)] = jnp.zeros((1, cols, 3 * ch), bf16)

    for copy in load_weight:
        copy.wait()
    load_sums = load(ema_sum_hbm, ema_sum, clips + 5 + taps)
    last = taps - 1
    send_stat2 = []
    for c in range(clips):
        rows_at_once = rows // PIECES
        for t in range(frames):
            for r in range(0, rows, rows_at_once):
                place = pl.ds(t * per_frame + r * cols, rows_at_once * cols)
                total = vid[c, t, r:r + rows_at_once].reshape(-1, ch).astype(f32)
                for a in range(taps):
                    from_frame = t + a - last
                    if from_frame < 0:
                        continue
                    left = jnp.concatenate(
                        [
                            wide[c, from_frame, r + b:r + b + rows_at_once].reshape(-1, 3 * ch)
                            for b in range(3)
                        ],
                        axis=1,
                    )
                    total = total + jnp.dot(left, weight[a].reshape(9 * ch, ch), preferred_element_type=f32)
                hid[c, place] = total

        def add(i, carry, c=c):
            v = hid[c, ds(i * block, block)]
            return carry[0] + fold(v), carry[1] + fold(v * v)

        zero = jnp.zeros((8, ch), f32)
        first, second = lax.fori_loop(0, per_clip // block, add, (zero, zero), unroll=True)
        stat2[c, 0:1] = first.sum(axis=0, keepdims=True)
        stat2[c, 1:2] = second.sum(axis=0, keepdims=True)
        send_stat2.append(push(stat2.at[c], got2.at[c], part_send.at[2 + c], part_recv.at[2 + c], partner))

    for c in range(1, clips):
        mark(c)
    send_count = push(count_own, count_core, cc_sem.at[0], cc_sem.at[1], other_core)

    far_half, own_half = ds((1 - core) * HALF, HALF), ds(core * HALF, HALF)
    for c in range(clips):
        send_stat2[c].wait()
        scale2, shift2 = affine(stat2[c] + got2[c], 1, gain2_ref)

        def second_act(i, carry, c=c):
            r = pl.multiple_of(i * block, block)
            act2[pl.ds(c * per_clip + r, block)] = act(hid[c, pl.ds(r, block)], scale2, shift2).astype(bf16)
            return carry

        lax.fori_loop(0, per_clip // block, second_act, 0)
        if c < clips - 1:
            mine = act2[c * per_clip:(c + 1) * per_clip]
            for i, place in enumerate((far_half, own_half)):
                part = jnp.dot(
                    member[place, c * per_clip:(c + 1) * per_clip], mine, preferred_element_type=f32
                )
                raw[i] = part if c == 0 else raw[i] + part

    def sums_of(i, w):
        start = ((1 - core) if i == 0 else core) * HALF + w * WAVE
        c = clips - 1
        mine = raw[i, w * WAVE:(w + 1) * WAVE]
        for k in range(c * per_clip, (c + 1) * per_clip, per_clip // 2):
            mine = mine + jnp.dot(
                member[ds(start, WAVE), k:k + per_clip // 2], act2[k:k + per_clip // 2], preferred_element_type=f32
            )
        high = mine.astype(bf16)
        low = (mine - high.astype(f32)).astype(bf16)
        return jnp.dot(high, proj_ref[...], preferred_element_type=f32) + jnp.dot(
            low, proj_ref[...], preferred_element_type=f32
        )

    send_core = []
    for w in range(WAVES):
        core_out[w] = sums_of(0, w).astype(bf16)
        send_core.append(push(core_out.at[w], core_in.at[w], core_send.at[w], core_recv.at[w], other_core))
    for w in range(WAVES):
        own = sums_of(1, w)
        send_core[w].wait()
        own = own + core_in[w].astype(f32)
        raw[1, w * WAVE:(w + 1) * WAVE] = own
        half[w] = own.astype(bf16)
        for i, peer in enumerate(plane_peers):
            push(half.at[w, ds(plane_chunks[i] * CHUNK, CHUNK)], plane_in.at[w, i], rs_send.at[w], rs_recv.at[w], peer)

    send_count.wait()
    count_chip[...] = count_own[...] + count_core[...]
    for i, peer in enumerate(plane_peers):
        push(count_chip, count_plane.at[i], cp_sem.at[0], cp_sem.at[1], peer)

    for w in range(WAVES):
        remote(plane_in.at[w], plane_in.at[w], rs_send.at[w], rs_recv.at[w], partner).wait()
        total = raw[1, ds(w * WAVE + own_chunk * CHUNK, CHUNK)]
        for i in range(NEAR):
            total = total + plane_in[w, i].astype(f32)
        z_buf[w, z] = total.astype(bf16)
        for peer in z_peers:
            push(z_buf.at[w, z], z_buf.at[w, z], z_send.at[w], z_recv.at[w], peer)

    load_sums.wait()
    smooth = smoothed(ema_count_ref[...])
    for j in range(CODES // SPAN):
        scale = jnp.concatenate([down(smooth[:, j * SPAN:(j + 1) * SPAN])] * (EMB // SPAN), axis=1)
        entry = ema_sum[j * SPAN:(j + 1) * SPAN] / scale
        high = entry.astype(bf16)
        book[j * SPAN:(j + 1) * SPAN, :EMB] = high
        book[j * SPAN:(j + 1) * SPAN, EMB:] = (entry - high.astype(f32)).astype(bf16)

    def distances(c):
        part = jnp.zeros((8, EMB), f32)
        for j in range(per_clip // 256):
            at = c * per_clip + j * 256
            picked = lax.dot_general(
                member[:, at:at + 256], book[...], (((0,), (0,)), ((), ())), preferred_element_type=f32
            )
            value = jnp.dot(act2[at:at + 256], proj_ref[...], preferred_element_type=f32)
            latent[at:at + 256] = value
            gap = value - (picked[:, :EMB] + picked[:, EMB:])
            part += fold(gap * gap)
        errs[pl.ds(c, 1)] = part.sum(axis=0, keepdims=True)

    for c in range(clips):
        distances(c)
    send_err = push(errs, got_err, part_send.at[2 + clips], part_recv.at[2 + clips], partner)

    every_count = remote(count_plane, count_plane, cp_sem.at[0], cp_sem.at[1], partner)
    every_count.wait()
    total = count_chip[...]
    for i in range(NEAR):
        total = total + count_plane[i]
    count_z[z] = total
    for peer in z_peers:
        push(count_z.at[z], count_z.at[z], cz_sem.at[0], cz_sem.at[1], peer)

    base = core * HALF
    for w in range(WAVES):
        arrived = z_buf.at[w, pl.ds(0, Z - 1)]
        remote(arrived, arrived, z_send.at[w], z_recv.at[w], partner).wait()
        total = z_buf[w, 0].astype(f32)
        for i in range(1, Z):
            total = total + z_buf[w, i].astype(f32)
        own_rows = ds(base + w * WAVE + own_chunk * CHUNK, CHUNK)
        sums_ref[own_rows] = total.astype(bf16)
        for peer in plane_peers:
            push(sums_ref.at[own_rows], sums_ref.at[own_rows], ag_send.at[w], ag_recv.at[w], peer)

    send_err.wait()
    err = (errs[...] + got_err[...]).sum(axis=1, keepdims=True) / (2 * per_clip * EMB)
    err_ref[...] = jnp.broadcast_to(err, err_ref.shape)

    forward = []
    for w in range(WAVES):
        remote(plane_in.at[w], plane_in.at[w], ag_send.at[w], ag_recv.at[w], partner).wait()
        here = ds(base + w * WAVE, WAVE)
        forward.append(push(sums_ref.at[here], sums_ref.at[here], fw_send.at[w], fw_recv.at[w], other_core))
    arrived = count_z.at[pl.ds(0, Z - 1)]
    remote(arrived, arrived, cz_sem.at[0], cz_sem.at[1], partner).wait()
    total = count_z[0]
    for i in range(1, Z):
        total = total + count_z[i]
    counts_ref[...] = total
    for copy in forward:
        copy.wait()


def finish(latent, ema_sum, sums, counts, err, ema_count, latent_hbm, book_hbm, count_ref, err_out, book, out_sem):
    parts = 4
    turn = CODES // parts
    write_latent = pltpu.make_async_copy(latent, latent_hbm, out_sem.at[parts])
    write_latent.start()
    code_count = DECAY * ema_count[...] + (1.0 - DECAY) * counts[...]
    count_ref[...] = code_count
    smooth = smoothed(code_count)
    for i in range(err_out.shape[0]):
        err_out[i] = err[i, 0]
    out = [write_latent]
    for i in range(parts):
        for j in range(i * turn // SPAN, (i + 1) * turn // SPAN):
            at = pl.ds(j * SPAN, SPAN)
            scale = jnp.concatenate([down(smooth[:, j * SPAN:(j + 1) * SPAN])] * (EMB // SPAN), axis=1)
            book[at] = (DECAY * ema_sum[at] + (1.0 - DECAY) * sums[at].astype(f32)) / scale
        at = pl.ds(i * turn, turn)
        copy = pltpu.make_async_copy(book.at[at], book_hbm.at[at], out_sem.at[i])
        copy.start()
        out.append(copy)
    for copy in out:
        copy.wait()


def body(video, gain_first, conv_weight, gain_second, proj_weight, codes, ema_sum, ema_count):
    clips, frames, rows, cols, ch = video.shape
    tokens = clips * frames * rows * cols
    taps = min(frames, conv_weight.shape[0])
    vmem = pl.BlockSpec(memory_space=pltpu.VMEM)
    hbm = pl.BlockSpec(memory_space=pltpu.HBM)
    dma = pltpu.SemaphoreType.DMA
    V = pltpu.VMEM
    count_row = ema_count.reshape(1, -1)
    keep = lambda a: pltpu.with_memory_space_constraint(a, pltpu.HBM)
    video, conv_weight, proj_weight, codes, ema_sum, count_row = map(keep, (video, conv_weight, proj_weight, codes, ema_sum, count_row))
    gain_first, gain_second = keep(gain_first.reshape(1,-1)), keep(gain_second.reshape(1,-1))
    latent, terms, sums, counts, err = pl.pallas_call(
        kernel,
        out_shape=(
            jax.ShapeDtypeStruct((tokens, EMB), f32),
            jax.ShapeDtypeStruct((CODES, EMB), f32),
            jax.ShapeDtypeStruct((CODES, EMB), bf16),
            jax.ShapeDtypeStruct((1, CODES), f32),
            jax.ShapeDtypeStruct((8, 128), f32),
        ),
        in_specs=[hbm] * 8,
        out_specs=(vmem,) * 5,
        scratch_shapes=[
            V(video.shape, bf16),
            V((clips, frames, 1, cols, ch), bf16),
            V((taps,) + conv_weight.shape[1:], bf16),
            V((clips, frames, rows + 2, cols, 3 * ch), bf16),
            V((clips, frames * rows * cols, ch), f32),
            V((tokens, ch), bf16),
            V((CODES, tokens), bf16),
            V((CODES, 2 * EMB), bf16),
            V((2, HALF, EMB), f32),
            V(codes.shape, jnp.int32),
            V((tokens // 128, 128), jnp.int32),
            V((1, ch), f32), V((1, ch), f32), V(proj_weight.shape, bf16), V((1, CODES), f32),
            V((8, ch), f32), V((clips, 8, ch), f32), V((8, ch), f32), V((clips, 8, ch), f32),
            V((8, EMB), f32), V((8, EMB), f32),
            V((1, CODES), f32), V((1, CODES), f32), V((1, CODES), f32),
            V((NEAR, 1, CODES), f32), V((Z, 1, CODES), f32),
            V((WAVES, WAVE, EMB), bf16), V((WAVES, WAVE, EMB), bf16), V((WAVES, WAVE, EMB), bf16),
            V((WAVES, NEAR, CHUNK, EMB), bf16), V((WAVES, Z, CHUNK, EMB), bf16),
            dma((clips + taps + 6,)),
            dma((clips + 3,)), dma((clips + 3,)), dma((2,)),
        ] + [dma((WAVES,))] * 10 + [dma((2,))] * 2,
        compiler_params=pltpu.CompilerParams(
            collective_id=0, has_side_effects=True, vmem_limit_bytes=32 << 20
        ),
    )(
        video, conv_weight, gain_first.reshape(1, -1), gain_second.reshape(1, -1), proj_weight,
        codes, ema_sum, count_row,
    )
    latent, codebook, code_count, clip_error = pl.pallas_call(
        finish,
        out_shape=(
            jax.ShapeDtypeStruct((tokens, EMB), f32),
            jax.ShapeDtypeStruct((CODES, EMB), f32),
            jax.ShapeDtypeStruct((1, CODES), f32),
            jax.ShapeDtypeStruct((clips,), f32),
        ),
        in_specs=[vmem] * 6,
        out_specs=(hbm, hbm, vmem, pl.BlockSpec(memory_space=pltpu.SMEM)),
        scratch_shapes=[
            V((CODES, EMB), f32), dma((5,)),
        ],
        compiler_params=pltpu.CompilerParams(vmem_limit_bytes=16 << 20),
    )(latent, terms, sums, counts, err, count_row)
    return (latent.reshape(video.shape[:4] + (EMB,)), codebook, code_count.reshape(-1), clip_error)


def solution(mesh):
    tiles = P("clip", None, "strip", None, None)
    in_specs = (tiles, P(), P(), P(), P(), P("clip", None, "strip", None), P(), P())
    out_specs = (tiles, P(), P(), P("clip"))
    return jax.shard_map(body, mesh=mesh, in_specs=in_specs, out_specs=out_specs, check_vma=False)
```

```python
import jax
import jax.numpy as jnp
from jax import lax
from jax.experimental import pallas as pl
from jax.experimental.pallas import tpu as pltpu
from jax.sharding import PartitionSpec as P

EMB = 256
CODES = 1024
GROUPS = 32
NORM_EPS = 1e-06
SMOOTH_EPS = 1e-05
DECAY = 0.9
MESH = pl.DeviceIdType.MESH

X, Y, Z, CORES = 4, 4, 8, 2
PLANE = X * Y
HALF = CODES // CORES
WAVES = 2
WAVE = HALF // WAVES
CHUNK = WAVE // PLANE
NEAR = PLANE - 1
SPAN = 128
CORE_PIECES = 1
PIECES = 2
bf16, f32 = jnp.bfloat16, jnp.float32


def address(x, y, z, core):
    return (((y // 2 * X + x) * Z + z) * CORES + core, y % 2)


def shifts():
    every = [(dx, dy) for dx in range(X) for dy in range(Y) if dx or dy]
    return sorted(every, key=lambda s: -(min(s[0], X - s[0]) + min(s[1], Y - s[1])))


def z_shifts():
    return sorted(range(1, Z), key=lambda d: -min(d, Z - d))


def ds(start, size):
    return pl.ds(pl.multiple_of(start, size), size)


def fold(v):
    return v.reshape(v.shape[0] // 8, 8, v.shape[1]).sum(axis=0)


def down(row):
    return jnp.broadcast_to(row, (SPAN, SPAN)).T


def smoothed(counts):
    grand = jnp.sum(counts)
    return (counts + SMOOTH_EPS) / (grand + CODES * SMOOTH_EPS) * grand


def kernel(
    video_hbm, weight_hbm, gain1_hbm, gain2_hbm, proj_hbm, codes_hbm, ema_sum_hbm, ema_count_hbm,
    latent, ema_sum, sums_ref, counts_ref, err_ref,
    vid, halo, weight, wide, hid, act2, member, book, raw, codes_in, codes_at,
    gain1_ref, gain2_ref, proj_ref, ema_count_ref,
    stat1, stat2, got1, got2, errs, got_err,
    count_own, count_core, count_chip, count_plane, count_z,
    core_out, core_in, half, plane_in, z_buf,
    load_sem, part_send, part_recv, cc_sem, core_send, core_recv,
    rs_send, rs_recv, z_send, z_recv, ag_send, ag_recv, fw_send, fw_recv,
    cp_sem, cz_sem,
):
    clips, frames, rows, cols, ch = vid.shape
    per_frame = rows * cols
    per_clip = frames * per_frame
    taps = weight.shape[0]
    skip = weight_hbm.shape[0] - taps

    def load(src, dst, i):
        copy = pltpu.make_async_copy(src, dst, load_sem.at[i])
        copy.start()
        return copy

    load_video = [load(video_hbm.at[c], vid.at[c], c) for c in range(clips)]
    load_codes = load(codes_hbm, codes_in, clips)
    load_small = [
        load(src, dst, clips + 1 + i)
        for i, (src, dst) in enumerate(
            [(gain1_hbm, gain1_ref), (gain2_hbm, gain2_ref), (ema_count_hbm, ema_count_ref), (proj_hbm, proj_ref)]
        )
    ]
    load_weight = [load(weight_hbm.at[skip + a], weight.at[a], clips + 5 + a) for a in range(taps)]

    clip, strip = lax.axis_index("clip"), lax.axis_index("strip")
    core = clip % CORES
    z = clip // CORES % Z
    x = clip // (CORES * Z) % X
    y = clip // (CORES * Z * X) * 2 + strip
    steps = shifts()
    z_steps = z_shifts()
    partner = (clip, 1 - strip)
    other_core = address(x, y, z, 1 - core)
    plane_peers = [address((x + dx) % X, (y + dy) % Y, z, core) for dx, dy in steps]
    plane_chunks = [(y + dy) % Y * X + (x + dx) % X for dx, dy in steps]
    from_chunks = [(y - dy + Y) % Y * X + (x - dx + X) % X for dx, dy in steps]
    own_chunk = y * X + x
    z_peers = [address(x, y, (z + d) % Z, core) for d in z_steps]

    barrier = pltpu.get_barrier_semaphore()
    direct = [i for i, (dx, dy) in enumerate(steps) if min(dx, X - dx) + min(dy, Y - dy) <= 1]
    cross = {i: address((x + steps[i][0]) % X, (y + steps[i][1]) % Y, z, 1 - core) for i in direct}
    everyone = plane_peers + z_peers + [other_core] + list(cross.values())
    for peer in everyone:
        pl.semaphore_signal(barrier, inc=1, device_id=peer, device_id_type=MESH)

    def remote(src, dst, send, recv, peer):
        return pltpu.make_async_remote_copy(
            src_ref=src, dst_ref=dst, send_sem=send, recv_sem=recv, device_id=peer, device_id_type=MESH
        )

    def push(src, dst, send, recv, peer):
        copy = remote(src, dst, send, recv, peer)
        copy.start()
        return copy

    block = 128
    lines = block // cols
    for ref in (stat1, stat2, errs):
        ref[...] = jnp.zeros_like(ref)
    for c in range(clips):
        load_video[c].wait()
        first = second = jnp.zeros((8, ch), f32)
        for t in range(frames):
            def add(i, carry, c=c, t=t):
                r = pl.multiple_of(i * lines, lines)
                v = vid[c, t, pl.ds(r, lines)].reshape(block, ch).astype(f32)
                return carry[0] + fold(v), carry[1] + fold(v * v)
            first, second = lax.fori_loop(0, per_frame // block, add, (first, second), unroll=True)
        stat1[pl.ds(c, 1)] = first.sum(axis=0, keepdims=True)
        stat1[pl.ds(clips + c, 1)] = second.sum(axis=0, keepdims=True)

    pl.semaphore_wait(barrier, len(everyone))
    send_stat1 = push(stat1, got1, part_send.at[0], part_recv.at[0], partner)
    edge = (rows - 1) * (1 - strip)
    send_halo = push(video_hbm.at[:, :, pl.ds(edge, 1)], halo, part_send.at[1], part_recv.at[1], partner)

    load_codes.wait()
    quads = rows // lines
    for c in range(clips):
        for t in range(frames):
            codes_at[pl.ds((c * frames + t) * quads, quads)] = jnp.concatenate(
                [codes_in[c, t, pl.ds(p, quads, stride=lines)] for p in range(lines)], axis=1
            )
    def mark(i, carry):
        k = pl.multiple_of(i * SPAN, SPAN)
        number = (lax.broadcasted_iota(jnp.int32, (SPAN, block), 0) + k).astype(jnp.int16)
        total = jnp.zeros((SPAN, block), bf16)
        for j in range(clips * frames * quads):
            hit = jnp.where(number == codes_at[j:j + 1].astype(jnp.int16), jnp.ones((), bf16), jnp.zeros((), bf16))
            total += hit
            member[pl.ds(k, SPAN), j * block:(j + 1) * block] = hit
        found = total.astype(f32).sum(axis=1, keepdims=True)
        count_own[:, pl.ds(k, SPAN)] = jnp.broadcast_to(found, (SPAN, SPAN)).T[:1]
        return carry

    lax.fori_loop(0, CODES // SPAN, mark, 0)
    send_count = push(count_own, count_core, cc_sem.at[0], cc_sem.at[1], other_core)

    members = per_clip * 2 * (ch // GROUPS)
    group = ch // GROUPS
    same = (
        lax.broadcasted_iota(jnp.int32, (ch, ch), 0) // group == lax.broadcasted_iota(jnp.int32, (ch, ch), 1) // group
    )
    ones = jnp.where(same, 1.0, 0.0).astype(f32)

    def affine(both, count, gain):
        grouped = jnp.dot(both, ones, precision=lax.Precision.HIGHEST, preferred_element_type=f32) / members
        centre, square = grouped[:count], grouped[count:2 * count]
        scale = lax.rsqrt(square - centre * centre + NORM_EPS) * gain[...]
        return scale, -centre * scale

    def act(v, scale, shift):
        h = v * (0.5 * scale) + 0.5 * shift
        return h + h * jnp.tanh(h)

    for copy in load_small:
        copy.wait()
    send_stat1.wait()
    scale1, shift1 = affine(stat1[...] + got1[...], clips, gain1_ref)

    def spread(v, put):
        col = lax.broadcasted_iota(jnp.int32, v.shape, 0) % cols
        put(0, jnp.where(col == 0, 0.0, pltpu.roll(v, 1, 0)).astype(bf16))
        put(1, v.astype(bf16))
        put(2, jnp.where(col == cols - 1, 0.0, pltpu.roll(v, v.shape[0] - 1, 0)).astype(bf16))

    for c in range(clips):
        for t in range(frames):
            def fill(i, carry, c=c, t=t):
                r = i * lines
                v = vid[c, t, pl.ds(r, lines)].reshape(block, ch).astype(f32)
                v = act(v, scale1[c:c + 1], shift1[c:c + 1])

                def put(e, w):
                    wide[c, t, pl.ds(r + 1, lines), :, e * ch:(e + 1) * ch] = w.reshape(lines, cols, ch)

                spread(v, put)
                return carry

            lax.fori_loop(0, rows // lines, fill, 0)

    send_halo.wait()
    near = (rows + 1) * (1 - strip)
    far = (rows + 1) * strip
    for c in range(clips):
        for t in range(frames):
            v = act(halo[c, t].reshape(cols, ch).astype(f32), scale1[c:c + 1], shift1[c:c + 1])

            def put(e, w, c=c, t=t):
                wide[c, t, pl.ds(near, 1), :, e * ch:(e + 1) * ch] = w.reshape(1, cols, ch)

            spread(v, put)
            wide[c, t, pl.ds(far, 1)] = jnp.zeros((1, cols, 3 * ch), bf16)

    for copy in load_weight:
        copy.wait()
    load_sums = load(ema_sum_hbm, ema_sum, clips + 5 + taps)
    last = taps - 1
    send_stat2 = []
    for c in range(clips):
        rows_at_once = rows // PIECES
        for t in range(frames):
            for r in range(0, rows, rows_at_once):
                place = pl.ds(t * per_frame + r * cols, rows_at_once * cols)
                total = vid[c, t, r:r + rows_at_once].reshape(-1, ch).astype(f32)
                for a in range(taps):
                    from_frame = t + a - last
                    if from_frame < 0:
                        continue
                    left = jnp.concatenate(
                        [
                            wide[c, from_frame, r + b:r + b + rows_at_once].reshape(-1, 3 * ch)
                            for b in range(3)
                        ],
                        axis=1,
                    )
                    total = total + jnp.dot(left, weight[a].reshape(9 * ch, ch), preferred_element_type=f32)
                hid[c, place] = total

        def add(i, carry, c=c):
            v = hid[c, ds(i * block, block)]
            return carry[0] + fold(v), carry[1] + fold(v * v)

        zero = jnp.zeros((8, ch), f32)
        first, second = lax.fori_loop(0, per_clip // block, add, (zero, zero), unroll=True)
        stat2[c, 0:1] = first.sum(axis=0, keepdims=True)
        stat2[c, 1:2] = second.sum(axis=0, keepdims=True)
        send_stat2.append(push(stat2.at[c], got2.at[c], part_send.at[2 + c], part_recv.at[2 + c], partner))

    send_count.wait()
    count_chip[...] = count_own[...] + count_core[...]
    for i, peer in enumerate(plane_peers):
        push(count_chip, count_plane.at[i], cp_sem.at[0], cp_sem.at[1], peer)

    far_half, own_half = ds((1 - core) * HALF, HALF), ds(core * HALF, HALF)
    for c in range(clips):
        send_stat2[c].wait()
        scale2, shift2 = affine(stat2[c] + got2[c], 1, gain2_ref)

        def second_act(i, carry, c=c):
            r = pl.multiple_of(i * block, block)
            act2[pl.ds(c * per_clip + r, block)] = act(hid[c, pl.ds(r, block)], scale2, shift2).astype(bf16)
            return carry

        lax.fori_loop(0, per_clip // block, second_act, 0)
        if c < clips - 1:
            mine = act2[c * per_clip:(c + 1) * per_clip]
            for i, place in enumerate((far_half, own_half)):
                part = jnp.dot(
                    member[place, c * per_clip:(c + 1) * per_clip], mine, preferred_element_type=f32
                )
                raw[i] = part if c == 0 else raw[i] + part

    def sums_of(i, w):
        start = ((1 - core) if i == 0 else core) * HALF + w * WAVE
        c = clips - 1
        mine = raw[i, w * WAVE:(w + 1) * WAVE]
        for k in range(c * per_clip, (c + 1) * per_clip, per_clip // 2):
            mine = mine + jnp.dot(
                member[ds(start, WAVE), k:k + per_clip // 2], act2[k:k + per_clip // 2], preferred_element_type=f32
            )
        return mine

    def projected(v):
        high = v.astype(bf16)
        low = (v - high.astype(f32)).astype(bf16)
        return jnp.dot(high, proj_ref[...], preferred_element_type=f32) + jnp.dot(
            low, proj_ref[...], preferred_element_type=f32
        )

    send_core = []
    outgoing = [sums_of(0, w).astype(bf16) for w in range(WAVES)]
    for w in range(WAVES):
        core_out[w] = outgoing[w]
    for w in range(WAVES):
        for p in range(CORE_PIECES):
            at = pl.ds(p * (WAVE // CORE_PIECES), WAVE // CORE_PIECES)
            push(core_out.at[w, at], core_in.at[w, at], core_send.at[w], core_recv.at[w], other_core)
    own = [sums_of(1, w) for w in range(WAVES)]
    for w in range(WAVES):
        remote(core_out.at[w], core_in.at[w], core_send.at[w], core_recv.at[w], other_core).wait()
        both = own[w] + core_in[w].astype(f32)
        raw[1, w * WAVE:(w + 1) * WAVE] = both
        half[w] = both.astype(bf16)
        for i, peer in enumerate(plane_peers):
            push(half.at[w, ds(plane_chunks[i] * CHUNK, CHUNK)], plane_in.at[w, i], rs_send.at[w], rs_recv.at[w], peer)

    for w in range(WAVES):
        remote(plane_in.at[w], plane_in.at[w], rs_send.at[w], rs_recv.at[w], partner).wait()
        total = raw[1, ds(w * WAVE + own_chunk * CHUNK, CHUNK)]
        for i in range(NEAR):
            total = total + plane_in[w, i].astype(f32)
        z_buf[w, z] = total.astype(bf16)
        for peer in z_peers:
            push(z_buf.at[w, z], z_buf.at[w, z], z_send.at[w], z_recv.at[w], peer)

    every_count = remote(count_plane, count_plane, cp_sem.at[0], cp_sem.at[1], partner)
    every_count.wait()
    total = count_chip[...]
    for i in range(NEAR):
        total = total + count_plane[i]
    count_z[z] = total
    for peer in z_peers:
        push(count_z.at[z], count_z.at[z], cz_sem.at[0], cz_sem.at[1], peer)

    load_sums.wait()
    smooth = smoothed(ema_count_ref[...])
    for j in range(CODES // SPAN):
        scale = jnp.concatenate([down(smooth[:, j * SPAN:(j + 1) * SPAN])] * (EMB // SPAN), axis=1)
        entry = ema_sum[j * SPAN:(j + 1) * SPAN] / scale
        high = entry.astype(bf16)
        book[j * SPAN:(j + 1) * SPAN, :EMB] = high
        book[j * SPAN:(j + 1) * SPAN, EMB:] = (entry - high.astype(f32)).astype(bf16)

    def distances(c):
        part = jnp.zeros((8, EMB), f32)
        for j in range(per_clip // 256):
            at = c * per_clip + j * 256
            picked = lax.dot_general(
                member[:, at:at + 256], book[...], (((0,), (0,)), ((), ())), preferred_element_type=f32
            )
            value = jnp.dot(act2[at:at + 256], proj_ref[...], preferred_element_type=f32)
            latent[at:at + 256] = value
            gap = value - (picked[:, :EMB] + picked[:, EMB:])
            part += fold(gap * gap)
        errs[pl.ds(c, 1)] = part.sum(axis=0, keepdims=True)

    for c in range(clips):
        distances(c)
    send_err = push(errs, got_err, part_send.at[2 + clips], part_recv.at[2 + clips], partner)

    base = core * HALF
    for w in range(WAVES):
        arrived = z_buf.at[w, pl.ds(0, Z - 1)]
        remote(arrived, arrived, z_send.at[w], z_recv.at[w], partner).wait()
        total = z_buf[w, 0].astype(f32)
        for i in range(1, Z):
            total = total + z_buf[w, i].astype(f32)
        own_rows = ds(base + w * WAVE + own_chunk * CHUNK, CHUNK)
        sums_ref[own_rows] = projected(total).astype(bf16)
        for i, peer in enumerate(plane_peers):
            push(sums_ref.at[own_rows], sums_ref.at[own_rows], ag_send.at[w], ag_recv.at[w, i], peer)
            if i in cross:
                push(sums_ref.at[own_rows], sums_ref.at[own_rows], fw_send.at[w], fw_recv.at[w], cross[i])
        push(sums_ref.at[own_rows], sums_ref.at[own_rows], fw_send.at[w], fw_recv.at[w], other_core)

    send_err.wait()
    err = (errs[...] + got_err[...]).sum(axis=1, keepdims=True) / (2 * per_clip * EMB)
    err_ref[...] = jnp.broadcast_to(err, err_ref.shape)

    for w in range(WAVES):
        for i in sorted(range(NEAR), key=lambda i: (i in cross, -i)):
            here = sums_ref.at[ds(base + w * WAVE + from_chunks[i] * CHUNK, CHUNK)]
            remote(here, here, ag_send.at[w], ag_recv.at[w, i], partner).wait_recv()
            if i not in cross:
                push(here, here, fw_send.at[w], fw_recv.at[w], other_core)
    arrived = count_z.at[pl.ds(0, Z - 1)]
    remote(arrived, arrived, cz_sem.at[0], cz_sem.at[1], partner).wait()
    total = count_z[0]
    for i in range(1, Z):
        total = total + count_z[i]
    counts_ref[...] = total
    for w in range(WAVES):
        remote(plane_in.at[w], plane_in.at[w], ag_send.at[w], fw_recv.at[w], partner).wait_send()
        mine = sums_ref.at[ds(base + w * WAVE, WAVE)]
        remote(mine, mine, fw_send.at[w], fw_recv.at[w], other_core).wait()


def finish(latent, ema_sum, sums, counts, err, ema_count, latent_hbm, book_hbm, count_ref, err_out, book, out_sem):
    parts = 4
    turn = CODES // parts
    write_latent = pltpu.make_async_copy(latent, latent_hbm, out_sem.at[parts])
    write_latent.start()
    code_count = DECAY * ema_count[...] + (1.0 - DECAY) * counts[...]
    count_ref[...] = code_count
    smooth = smoothed(code_count)
    for i in range(err_out.shape[0]):
        err_out[i] = err[i, 0]
    out = [write_latent]
    for i in range(parts):
        for j in range(i * turn // SPAN, (i + 1) * turn // SPAN):
            at = pl.ds(j * SPAN, SPAN)
            scale = jnp.concatenate([down(smooth[:, j * SPAN:(j + 1) * SPAN])] * (EMB // SPAN), axis=1)
            book[at] = (DECAY * ema_sum[at] + (1.0 - DECAY) * sums[at].astype(f32)) / scale
        at = pl.ds(i * turn, turn)
        copy = pltpu.make_async_copy(book.at[at], book_hbm.at[at], out_sem.at[i])
        copy.start()
        out.append(copy)
    for copy in out:
        copy.wait()


def body(video, gain_first, conv_weight, gain_second, proj_weight, codes, ema_sum, ema_count):
    clips, frames, rows, cols, ch = video.shape
    tokens = clips * frames * rows * cols
    taps = min(frames, conv_weight.shape[0])
    vmem = pl.BlockSpec(memory_space=pltpu.VMEM)
    hbm = pl.BlockSpec(memory_space=pltpu.HBM)
    dma = pltpu.SemaphoreType.DMA
    V = pltpu.VMEM
    count_row = ema_count.reshape(1, -1)
    keep = lambda a: pltpu.with_memory_space_constraint(a, pltpu.HBM)
    video, conv_weight, proj_weight, codes, ema_sum, count_row = map(keep, (video, conv_weight, proj_weight, codes, ema_sum, count_row))
    gain_first, gain_second = keep(gain_first.reshape(1,-1)), keep(gain_second.reshape(1,-1))
    latent, terms, sums, counts, err = pl.pallas_call(
        kernel,
        out_shape=(
            jax.ShapeDtypeStruct((tokens, EMB), f32),
            jax.ShapeDtypeStruct((CODES, EMB), f32),
            jax.ShapeDtypeStruct((CODES, EMB), bf16),
            jax.ShapeDtypeStruct((1, CODES), f32),
            jax.ShapeDtypeStruct((8, 128), f32),
        ),
        in_specs=[hbm] * 8,
        out_specs=(vmem,) * 5,
        scratch_shapes=[
            V(video.shape, bf16),
            V((clips, frames, 1, cols, ch), bf16),
            V((taps,) + conv_weight.shape[1:], bf16),
            V((clips, frames, rows + 2, cols, 3 * ch), bf16),
            V((clips, frames * rows * cols, ch), f32),
            V((tokens, ch), bf16),
            V((CODES, tokens), bf16),
            V((CODES, 2 * EMB), bf16),
            V((2, HALF, EMB), f32),
            V(codes.shape, jnp.int32),
            V((tokens // 128, 128), jnp.int32),
            V((1, ch), f32), V((1, ch), f32), V(proj_weight.shape, bf16), V((1, CODES), f32),
            V((8, ch), f32), V((clips, 8, ch), f32), V((8, ch), f32), V((clips, 8, ch), f32),
            V((8, EMB), f32), V((8, EMB), f32),
            V((1, CODES), f32), V((1, CODES), f32), V((1, CODES), f32),
            V((NEAR, 1, CODES), f32), V((Z, 1, CODES), f32),
            V((WAVES, WAVE, EMB), bf16), V((WAVES, WAVE, EMB), bf16), V((WAVES, WAVE, EMB), bf16),
            V((WAVES, NEAR, CHUNK, EMB), bf16), V((WAVES, Z, CHUNK, EMB), bf16),
            dma((clips + taps + 6,)),
            dma((clips + 3,)), dma((clips + 3,)), dma((2,)),
        ] + [dma((WAVES,))] * 7 + [dma((WAVES, NEAR))] + [dma((WAVES,))] * 2 + [dma((2,))] * 2,
        compiler_params=pltpu.CompilerParams(
            collective_id=0, has_side_effects=True, vmem_limit_bytes=32 << 20
        ),
    )(
        video, conv_weight, gain_first.reshape(1, -1), gain_second.reshape(1, -1), proj_weight,
        codes, ema_sum, count_row,
    )
    latent, codebook, code_count, clip_error = pl.pallas_call(
        finish,
        out_shape=(
            jax.ShapeDtypeStruct((tokens, EMB), f32),
            jax.ShapeDtypeStruct((CODES, EMB), f32),
            jax.ShapeDtypeStruct((1, CODES), f32),
            jax.ShapeDtypeStruct((clips,), f32),
        ),
        in_specs=[vmem] * 6,
        out_specs=(hbm, hbm, vmem, pl.BlockSpec(memory_space=pltpu.SMEM)),
        scratch_shapes=[
            V((CODES, EMB), f32), dma((5,)),
        ],
        compiler_params=pltpu.CompilerParams(vmem_limit_bytes=16 << 20),
    )(latent, terms, sums, counts, err, count_row)
    return (latent.reshape(video.shape[:4] + (EMB,)), codebook, code_count.reshape(-1), clip_error)


def solution(mesh):
    tiles = P("clip", None, "strip", None, None)
    in_specs = (tiles, P(), P(), P(), P(), P("clip", None, "strip", None), P(), P())
    out_specs = (tiles, P(), P(), P("clip"))
    return jax.shard_map(body, mesh=mesh, in_specs=in_specs, out_specs=out_specs, check_vma=False)
```

```python
import jax
import jax.numpy as jnp
from jax import lax
from jax.experimental import pallas as pl
from jax.experimental.pallas import tpu as pltpu
from jax.sharding import PartitionSpec as P

EMB = 256
CODES = 1024
GROUPS = 32
NORM_EPS = 1e-06
SMOOTH_EPS = 1e-05
DECAY = 0.9
MESH = pl.DeviceIdType.MESH

X, Y, Z, CORES = 4, 4, 8, 2
PLANE = X * Y
HALF = CODES // CORES
WAVES = 2
WAVE = HALF // WAVES
CHUNK = WAVE // PLANE
NEAR = PLANE - 1
SPAN = 128
PIECES = 4
bf16, f32 = jnp.bfloat16, jnp.float32


def address(x, y, z, core):
    return (((y // 2 * X + x) * Z + z) * CORES + core, y % 2)


def shifts():
    every = [(dx, dy) for dx in range(X) for dy in range(Y) if dx or dy]
    return sorted(every, key=lambda s: -(min(s[0], X - s[0]) + min(s[1], Y - s[1])))


def z_shifts():
    return sorted(range(1, Z), key=lambda d: -min(d, Z - d))


def ds(start, size):
    return pl.ds(pl.multiple_of(start, size), size)


def fold(v):
    return v.reshape(v.shape[0] // 8, 8, v.shape[1]).sum(axis=0)


def down(row):
    return jnp.broadcast_to(row, (SPAN, SPAN)).T


def smoothed(counts):
    grand = jnp.sum(counts)
    return (counts + SMOOTH_EPS) / (grand + CODES * SMOOTH_EPS) * grand


def kernel(
    video_hbm, weight_hbm, gain1_hbm, gain2_hbm, proj_hbm, codes_hbm, ema_sum_hbm, ema_count_hbm,
    latent, ema_sum, sums_ref, counts_ref, err_ref,
    vid, halo, weight, wide, hid, act2, member, book, raw, codes_in, codes_at,
    gain1_ref, gain2_ref, proj_ref, ema_count_ref,
    stat1, stat2, got1, got2, errs, got_err,
    count_own, count_core, count_chip, count_plane, count_z,
    core_out, core_in, half, plane_in, z_buf,
    load_sem, part_send, part_recv, cc_sem, core_send, core_recv,
    rs_send, rs_recv, z_send, z_recv, ag_send, ag_recv, fw_send, fw_recv,
    cp_sem, cz_sem,
):
    clips, frames, rows, cols, ch = vid.shape
    per_frame = rows * cols
    per_clip = frames * per_frame
    taps = weight.shape[0]
    skip = weight_hbm.shape[0] - taps

    def load(src, dst, i):
        copy = pltpu.make_async_copy(src, dst, load_sem.at[i])
        copy.start()
        return copy

    load_video = [load(video_hbm.at[c], vid.at[c], c) for c in range(clips)]
    load_codes = load(codes_hbm, codes_in, clips)
    load_small = [
        load(src, dst, clips + 1 + i)
        for i, (src, dst) in enumerate(
            [(gain1_hbm, gain1_ref), (gain2_hbm, gain2_ref), (ema_count_hbm, ema_count_ref), (proj_hbm, proj_ref)]
        )
    ]
    load_weight = [load(weight_hbm.at[skip + a], weight.at[a], clips + 5 + a) for a in range(taps)]

    clip, strip = lax.axis_index("clip"), lax.axis_index("strip")
    core = clip % CORES
    z = clip // CORES % Z
    x = clip // (CORES * Z) % X
    y = clip // (CORES * Z * X) * 2 + strip
    steps = shifts()
    z_steps = z_shifts()
    partner = (clip, 1 - strip)
    other_core = address(x, y, z, 1 - core)
    plane_peers = [address((x + dx) % X, (y + dy) % Y, z, core) for dx, dy in steps]
    plane_chunks = [(y + dy) % Y * X + (x + dx) % X for dx, dy in steps]
    from_chunks = [(y - dy + Y) % Y * X + (x - dx + X) % X for dx, dy in steps]
    own_chunk = y * X + x
    z_peers = [address(x, y, (z + d) % Z, core) for d in z_steps]

    barrier = pltpu.get_barrier_semaphore()
    direct = [i for i, (dx, dy) in enumerate(steps) if min(dx, X - dx) + min(dy, Y - dy) <= 1]
    cross = {i: address((x + steps[i][0]) % X, (y + steps[i][1]) % Y, z, 1 - core) for i in direct}
    everyone = plane_peers + z_peers + [other_core] + list(cross.values())
    for peer in everyone:
        pl.semaphore_signal(barrier, inc=1, device_id=peer, device_id_type=MESH)

    def remote(src, dst, send, recv, peer):
        return pltpu.make_async_remote_copy(
            src_ref=src, dst_ref=dst, send_sem=send, recv_sem=recv, device_id=peer, device_id_type=MESH
        )

    def push(src, dst, send, recv, peer):
        copy = remote(src, dst, send, recv, peer)
        copy.start()
        return copy

    block = 128
    lines = block // cols
    for ref in (stat1, stat2, errs):
        ref[...] = jnp.zeros_like(ref)
    for c in range(clips):
        load_video[c].wait()
        first = second = jnp.zeros((8, ch), f32)
        for t in range(frames):
            def add(i, carry, c=c, t=t):
                r = pl.multiple_of(i * lines, lines)
                v = vid[c, t, pl.ds(r, lines)].reshape(block, ch).astype(f32)
                return carry[0] + fold(v), carry[1] + fold(v * v)
            first, second = lax.fori_loop(0, per_frame // block, add, (first, second), unroll=True)
        stat1[pl.ds(c, 1)] = first.sum(axis=0, keepdims=True)
        stat1[pl.ds(clips + c, 1)] = second.sum(axis=0, keepdims=True)

    pl.semaphore_wait(barrier, len(everyone))
    send_stat1 = push(stat1, got1, part_send.at[0], part_recv.at[0], partner)
    edge = (rows - 1) * (1 - strip)
    send_halo = push(video_hbm.at[:, :, pl.ds(edge, 1)], halo, part_send.at[1], part_recv.at[1], partner)

    load_codes.wait()
    quads = rows // lines
    for c in range(clips):
        for t in range(frames):
            codes_at[pl.ds((c * frames + t) * quads, quads)] = jnp.concatenate(
                [codes_in[c, t, pl.ds(p, quads, stride=lines)] for p in range(lines)], axis=1
            )
    def mark(i, carry):
        k = pl.multiple_of(i * SPAN, SPAN)
        number = (lax.broadcasted_iota(jnp.int32, (SPAN, block), 0) + k).astype(jnp.int16)
        total = jnp.zeros((SPAN, block), bf16)
        for j in range(clips * frames * quads):
            hit = jnp.where(number == codes_at[j:j + 1].astype(jnp.int16), jnp.ones((), bf16), jnp.zeros((), bf16))
            total += hit
            member[pl.ds(k, SPAN), j * block:(j + 1) * block] = hit
        found = total.astype(f32).sum(axis=1, keepdims=True)
        count_own[:, pl.ds(k, SPAN)] = jnp.broadcast_to(found, (SPAN, SPAN)).T[:1]
        return carry

    lax.fori_loop(0, CODES // SPAN, mark, 0)
    send_count = push(count_own, count_core, cc_sem.at[0], cc_sem.at[1], other_core)

    members = per_clip * 2 * (ch // GROUPS)
    group = ch // GROUPS
    same = (
        lax.broadcasted_iota(jnp.int32, (ch, ch), 0) // group == lax.broadcasted_iota(jnp.int32, (ch, ch), 1) // group
    )
    ones = jnp.where(same, 1.0, 0.0).astype(f32)

    def affine(both, count, gain):
        grouped = jnp.dot(both, ones, precision=lax.Precision.HIGHEST, preferred_element_type=f32) / members
        centre, square = grouped[:count], grouped[count:2 * count]
        scale = lax.rsqrt(square - centre * centre + NORM_EPS) * gain[...]
        return scale, -centre * scale

    def act(v, scale, shift):
        h = v * (0.5 * scale) + 0.5 * shift
        return h + h * jnp.tanh(h)

    for copy in load_small:
        copy.wait()
    send_stat1.wait()
    scale1, shift1 = affine(stat1[...] + got1[...], clips, gain1_ref)

    def spread(v, put):
        col = lax.broadcasted_iota(jnp.int32, v.shape, 0) % cols
        put(0, jnp.where(col == 0, 0.0, pltpu.roll(v, 1, 0)).astype(bf16))
        put(1, v.astype(bf16))
        put(2, jnp.where(col == cols - 1, 0.0, pltpu.roll(v, v.shape[0] - 1, 0)).astype(bf16))

    for c in range(clips):
        for t in range(frames):
            def fill(i, carry, c=c, t=t):
                r = i * lines
                v = vid[c, t, pl.ds(r, lines)].reshape(block, ch).astype(f32)
                v = act(v, scale1[c:c + 1], shift1[c:c + 1])

                def put(e, w):
                    wide[c, t, pl.ds(r + 1, lines), :, e * ch:(e + 1) * ch] = w.reshape(lines, cols, ch)

                spread(v, put)
                return carry

            lax.fori_loop(0, rows // lines, fill, 0)

    send_halo.wait()
    near = (rows + 1) * (1 - strip)
    far = (rows + 1) * strip
    for c in range(clips):
        for t in range(frames):
            v = act(halo[c, t].reshape(cols, ch).astype(f32), scale1[c:c + 1], shift1[c:c + 1])

            def put(e, w, c=c, t=t):
                wide[c, t, pl.ds(near, 1), :, e * ch:(e + 1) * ch] = w.reshape(1, cols, ch)

            spread(v, put)
            wide[c, t, pl.ds(far, 1)] = jnp.zeros((1, cols, 3 * ch), bf16)

    for copy in load_weight:
        copy.wait()
    load_sums = load(ema_sum_hbm, ema_sum, clips + 5 + taps)
    last = taps - 1
    send_stat2 = []
    for c in range(clips):
        rows_at_once = rows // PIECES
        for t in range(frames):
            for r in range(0, rows, rows_at_once):
                place = pl.ds(t * per_frame + r * cols, rows_at_once * cols)
                total = vid[c, t, r:r + rows_at_once].reshape(-1, ch).astype(f32)
                for a in range(taps):
                    from_frame = t + a - last
                    if from_frame < 0:
                        continue
                    left = jnp.concatenate(
                        [
                            wide[c, from_frame, r + b:r + b + rows_at_once].reshape(-1, 3 * ch)
                            for b in range(3)
                        ],
                        axis=1,
                    )
                    total = total + jnp.dot(left, weight[a].reshape(9 * ch, ch), preferred_element_type=f32)
                hid[c, place] = total

        def add(i, carry, c=c):
            v = hid[c, ds(i * block, block)]
            return carry[0] + fold(v), carry[1] + fold(v * v)

        zero = jnp.zeros((8, ch), f32)
        first, second = lax.fori_loop(0, per_clip // block, add, (zero, zero), unroll=True)
        stat2[c, 0:1] = first.sum(axis=0, keepdims=True)
        stat2[c, 1:2] = second.sum(axis=0, keepdims=True)
        send_stat2.append(push(stat2.at[c], got2.at[c], part_send.at[2 + c], part_recv.at[2 + c], partner))

    send_count.wait()
    count_chip[...] = count_own[...] + count_core[...]
    for i, peer in enumerate(plane_peers):
        push(count_chip, count_plane.at[i], cp_sem.at[0], cp_sem.at[1], peer)

    far_half, own_half = ds((1 - core) * HALF, HALF), ds(core * HALF, HALF)
    for c in range(clips):
        send_stat2[c].wait()
        scale2, shift2 = affine(stat2[c] + got2[c], 1, gain2_ref)

        def second_act(i, carry, c=c):
            r = pl.multiple_of(i * block, block)
            act2[pl.ds(c * per_clip + r, block)] = act(hid[c, pl.ds(r, block)], scale2, shift2).astype(bf16)
            return carry

        lax.fori_loop(0, per_clip // block, second_act, 0)
        if c < clips - 1:
            mine = act2[c * per_clip:(c + 1) * per_clip]
            for i, place in enumerate((far_half, own_half)):
                part = jnp.dot(
                    member[place, c * per_clip:(c + 1) * per_clip], mine, preferred_element_type=f32
                )
                raw[i] = part if c == 0 else raw[i] + part

    def sums_of(i, w):
        start = ((1 - core) if i == 0 else core) * HALF + w * WAVE
        c = clips - 1
        mine = raw[i, w * WAVE:(w + 1) * WAVE]
        for k in range(c * per_clip, (c + 1) * per_clip, per_clip // 2):
            mine = mine + jnp.dot(
                member[ds(start, WAVE), k:k + per_clip // 2], act2[k:k + per_clip // 2], preferred_element_type=f32
            )
        return mine

    def projected(v):
        high = v.astype(bf16)
        low = (v - high.astype(f32)).astype(bf16)
        return jnp.dot(high, proj_ref[...], preferred_element_type=f32) + jnp.dot(
            low, proj_ref[...], preferred_element_type=f32
        )

    send_core = []
    for w in range(WAVES):
        core_out[w] = sums_of(0, w).astype(bf16)
        push(core_out.at[w], core_in.at[w], core_send.at[w], core_recv.at[w], other_core)
    own = [sums_of(1, w) for w in range(WAVES)]
    for w in range(WAVES):
        remote(core_out.at[w], core_in.at[w], core_send.at[w], core_recv.at[w], other_core).wait()
        both = own[w] + core_in[w].astype(f32)
        raw[1, w * WAVE:(w + 1) * WAVE] = both
        half[w] = both.astype(bf16)
        for i, peer in enumerate(plane_peers):
            push(half.at[w, ds(plane_chunks[i] * CHUNK, CHUNK)], plane_in.at[w, i], rs_send.at[w], rs_recv.at[w], peer)

    for w in range(WAVES):
        remote(plane_in.at[w], plane_in.at[w], rs_send.at[w], rs_recv.at[w], partner).wait()
        total = raw[1, ds(w * WAVE + own_chunk * CHUNK, CHUNK)]
        for i in range(NEAR):
            total = total + plane_in[w, i].astype(f32)
        z_buf[w, z] = total.astype(bf16)
        for peer in z_peers:
            push(z_buf.at[w, z], z_buf.at[w, z], z_send.at[w], z_recv.at[w], peer)

    every_count = remote(count_plane, count_plane, cp_sem.at[0], cp_sem.at[1], partner)
    every_count.wait()
    total = count_chip[...]
    for i in range(NEAR):
        total = total + count_plane[i]
    count_z[z] = total
    for peer in z_peers:
        push(count_z.at[z], count_z.at[z], cz_sem.at[0], cz_sem.at[1], peer)

    load_sums.wait()
    smooth = smoothed(ema_count_ref[...])
    for j in range(CODES // SPAN):
        scale = jnp.concatenate([down(smooth[:, j * SPAN:(j + 1) * SPAN])] * (EMB // SPAN), axis=1)
        entry = ema_sum[j * SPAN:(j + 1) * SPAN] / scale
        high = entry.astype(bf16)
        book[j * SPAN:(j + 1) * SPAN, :EMB] = high
        book[j * SPAN:(j + 1) * SPAN, EMB:] = (entry - high.astype(f32)).astype(bf16)

    def distances(c):
        part = jnp.zeros((8, EMB), f32)
        for j in range(per_clip // 256):
            at = c * per_clip + j * 256
            picked = lax.dot_general(
                member[:, at:at + 256], book[...], (((0,), (0,)), ((), ())), preferred_element_type=f32
            )
            value = jnp.dot(act2[at:at + 256], proj_ref[...], preferred_element_type=f32)
            latent[at:at + 256] = value
            gap = value - (picked[:, :EMB] + picked[:, EMB:])
            part += fold(gap * gap)
        errs[pl.ds(c, 1)] = part.sum(axis=0, keepdims=True)

    for c in range(clips):
        distances(c)
    send_err = push(errs, got_err, part_send.at[2 + clips], part_recv.at[2 + clips], partner)

    base = core * HALF
    for w in range(WAVES):
        arrived = z_buf.at[w, pl.ds(0, Z - 1)]
        remote(arrived, arrived, z_send.at[w], z_recv.at[w], partner).wait()
        total = z_buf[w, 0].astype(f32)
        for i in range(1, Z):
            total = total + z_buf[w, i].astype(f32)
        own_rows = ds(base + w * WAVE + own_chunk * CHUNK, CHUNK)
        sums_ref[own_rows] = projected(total).astype(bf16)
        for i, peer in enumerate(plane_peers):
            push(sums_ref.at[own_rows], sums_ref.at[own_rows], ag_send.at[w], ag_recv.at[w, i], peer)
            if i in cross:
                push(sums_ref.at[own_rows], sums_ref.at[own_rows], fw_send.at[w], fw_recv.at[w], cross[i])
        push(sums_ref.at[own_rows], sums_ref.at[own_rows], fw_send.at[w], fw_recv.at[w], other_core)

    send_err.wait()
    err = (errs[...] + got_err[...]).sum(axis=1, keepdims=True) / (2 * per_clip * EMB)
    err_ref[...] = jnp.broadcast_to(err, err_ref.shape)

    for w in range(WAVES):
        for i in sorted(range(NEAR), key=lambda i: (i in cross, -i)):
            here = sums_ref.at[ds(base + w * WAVE + from_chunks[i] * CHUNK, CHUNK)]
            remote(here, here, ag_send.at[w], ag_recv.at[w, i], partner).wait_recv()
            if i not in cross:
                push(here, here, fw_send.at[w], fw_recv.at[w], other_core)
    arrived = count_z.at[pl.ds(0, Z - 1)]
    remote(arrived, arrived, cz_sem.at[0], cz_sem.at[1], partner).wait()
    total = count_z[0]
    for i in range(1, Z):
        total = total + count_z[i]
    counts_ref[...] = total
    for w in range(WAVES):
        remote(plane_in.at[w], plane_in.at[w], ag_send.at[w], fw_recv.at[w], partner).wait_send()
        mine = sums_ref.at[ds(base + w * WAVE, WAVE)]
        remote(mine, mine, fw_send.at[w], fw_recv.at[w], other_core).wait()


def finish(latent, ema_sum, sums, counts, err, ema_count, latent_hbm, book_hbm, count_ref, err_out, book, out_sem):
    parts = 4
    turn = CODES // parts
    write_latent = pltpu.make_async_copy(latent, latent_hbm, out_sem.at[parts])
    write_latent.start()
    code_count = DECAY * ema_count[...] + (1.0 - DECAY) * counts[...]
    count_ref[...] = code_count
    smooth = smoothed(code_count)
    for i in range(err_out.shape[0]):
        err_out[i] = err[i, 0]
    out = [write_latent]
    for i in range(parts):
        for j in range(i * turn // SPAN, (i + 1) * turn // SPAN):
            at = pl.ds(j * SPAN, SPAN)
            scale = jnp.concatenate([down(smooth[:, j * SPAN:(j + 1) * SPAN])] * (EMB // SPAN), axis=1)
            book[at] = (DECAY * ema_sum[at] + (1.0 - DECAY) * sums[at].astype(f32)) / scale
        at = pl.ds(i * turn, turn)
        copy = pltpu.make_async_copy(book.at[at], book_hbm.at[at], out_sem.at[i])
        copy.start()
        out.append(copy)
    for copy in out:
        copy.wait()


def body(video, gain_first, conv_weight, gain_second, proj_weight, codes, ema_sum, ema_count):
    clips, frames, rows, cols, ch = video.shape
    tokens = clips * frames * rows * cols
    taps = min(frames, conv_weight.shape[0])
    vmem = pl.BlockSpec(memory_space=pltpu.VMEM)
    hbm = pl.BlockSpec(memory_space=pltpu.HBM)
    dma = pltpu.SemaphoreType.DMA
    V = pltpu.VMEM
    count_row = ema_count.reshape(1, -1)
    keep = lambda a: pltpu.with_memory_space_constraint(a, pltpu.HBM)
    video, conv_weight, proj_weight, codes, ema_sum, count_row = map(keep, (video, conv_weight, proj_weight, codes, ema_sum, count_row))
    gain_first, gain_second = keep(gain_first.reshape(1,-1)), keep(gain_second.reshape(1,-1))
    latent, terms, sums, counts, err = pl.pallas_call(
        kernel,
        out_shape=(
            jax.ShapeDtypeStruct((tokens, EMB), f32),
            jax.ShapeDtypeStruct((CODES, EMB), f32),
            jax.ShapeDtypeStruct((CODES, EMB), bf16),
            jax.ShapeDtypeStruct((1, CODES), f32),
            jax.ShapeDtypeStruct((8, 128), f32),
        ),
        in_specs=[hbm] * 8,
        out_specs=(vmem,) * 5,
        scratch_shapes=[
            V(video.shape, bf16),
            V((clips, frames, 1, cols, ch), bf16),
            V((taps,) + conv_weight.shape[1:], bf16),
            V((clips, frames, rows + 2, cols, 3 * ch), bf16),
            V((clips, frames * rows * cols, ch), f32),
            V((tokens, ch), bf16),
            V((CODES, tokens), bf16),
            V((CODES, 2 * EMB), bf16),
            V((2, HALF, EMB), f32),
            V(codes.shape, jnp.int32),
            V((tokens // 128, 128), jnp.int32),
            V((1, ch), f32), V((1, ch), f32), V(proj_weight.shape, bf16), V((1, CODES), f32),
            V((8, ch), f32), V((clips, 8, ch), f32), V((8, ch), f32), V((clips, 8, ch), f32),
            V((8, EMB), f32), V((8, EMB), f32),
            V((1, CODES), f32), V((1, CODES), f32), V((1, CODES), f32),
            V((NEAR, 1, CODES), f32), V((Z, 1, CODES), f32),
            V((WAVES, WAVE, EMB), bf16), V((WAVES, WAVE, EMB), bf16), V((WAVES, WAVE, EMB), bf16),
            V((WAVES, NEAR, CHUNK, EMB), bf16), V((WAVES, Z, CHUNK, EMB), bf16),
            dma((clips + taps + 6,)),
            dma((clips + 3,)), dma((clips + 3,)), dma((2,)),
        ] + [dma((WAVES,))] * 7 + [dma((WAVES, NEAR))] + [dma((WAVES,))] * 2 + [dma((2,))] * 2,
        compiler_params=pltpu.CompilerParams(
            collective_id=0, has_side_effects=True, vmem_limit_bytes=32 << 20
        ),
    )(
        video, conv_weight, gain_first.reshape(1, -1), gain_second.reshape(1, -1), proj_weight,
        codes, ema_sum, count_row,
    )
    latent, codebook, code_count, clip_error = pl.pallas_call(
        finish,
        out_shape=(
            jax.ShapeDtypeStruct((tokens, EMB), f32),
            jax.ShapeDtypeStruct((CODES, EMB), f32),
            jax.ShapeDtypeStruct((1, CODES), f32),
            jax.ShapeDtypeStruct((clips,), f32),
        ),
        in_specs=[vmem] * 6,
        out_specs=(hbm, hbm, vmem, pl.BlockSpec(memory_space=pltpu.SMEM)),
        scratch_shapes=[
            V((CODES, EMB), f32), dma((5,)),
        ],
        compiler_params=pltpu.CompilerParams(vmem_limit_bytes=16 << 20),
    )(latent, terms, sums, counts, err, count_row)
    return (latent.reshape(video.shape[:4] + (EMB,)), codebook, code_count.reshape(-1), clip_error)


def solution(mesh):
    tiles = P("clip", None, "strip", None, None)
    in_specs = (tiles, P(), P(), P(), P(), P("clip", None, "strip", None), P(), P())
    out_specs = (tiles, P(), P(), P("clip"))
    return jax.shard_map(body, mesh=mesh, in_specs=in_specs, out_specs=out_specs, check_vma=False)
```
